256 devices in a mesh: sec: 2 (over x_lo), slab: 64 (over z, y, core), ch: 2 (over x_hi).
Axes of the slice: x: 4 (x_hi: 2, x_lo: 2; x = x_hi * 2 + x_lo), y: 4, z: 8, core: 2. Of those that a mesh axis runs over, the one named last changes fastest.
Arguments:
- latents: bfloat16 [4, 64, 64, 16], P('sec', None, 'slab'), may hold values from -6 to 6
- weight_in: bfloat16 [3, 3, 3, 16, 384], replicated, may hold values from -0.3125 to 0.3125
- weight_mid: bfloat16 [3, 3, 3, 384, 384], replicated, may hold values from -0.0625 to 0.0625
- weight_up: bfloat16 [3, 3, 3, 384, 192], replicated, may hold values from -0.0625 to 0.0625
- reward_grad: bfloat16 [4, 128, 128, 192], P('sec', 'slab', None, 'ch'), may hold values from -6 to 6
Outputs:
- decoded: bfloat16 [4, 128, 128, 192], P('sec', 'slab', None, 'ch')
- latent_grad: float32 [4, 64, 64, 16], P('sec', None, 'slab')
The draws below stay inside these ranges and needn't reach their ends.
All inputs are finite; a program needn't handle non-finite values.
Results may differ from the reference program's by a relative error of at most 0.0052.
Values may be sent and summed in bfloat16 or wider, within the bound.
A program may use at most 128 MiB of HBM per device.

```python
import jax
import jax.numpy as jnp
from jax import lax

C_LAT = 16
C1 = 384
C2 = 192
W = 64
F = 4
H = 64


def block_levels(stream_key, shape, split, least, top_value):
    loudness, own = 1.0, jax.random.fold_in(stream_key, 6)
    for dim, parts in split:
        steps = jnp.exp(jax.random.uniform(jax.random.fold_in(own, dim), (parts,), jnp.float32, least / len(split), top_value / len(split)))
        loudness = loudness * jnp.repeat(steps, shape[dim] // parts).reshape([-1 if axis == dim else 1 for axis in range(len(shape))])
    return loudness


def gaussian(stream_key, shape, scale, reach, shards=(), kind=jnp.bfloat16):
    values = jax.random.normal(stream_key, shape, jnp.float32) * scale
    if len(shards) > 0:
        values = block_levels(stream_key, shape, shards, -0.22, 0.18) * values
    return jnp.clip(values, min=-reach, max=reach).astype(kind)


def setup_inputs(seed: int = 0) -> dict:
    seeds = jax.random.split(jax.random.key(seed), 6)
    latents = gaussian(seeds[0], (F, H, W, C_LAT), 1.0, 6.0, ((0, 2), (2, 64)))
    weight_in = gaussian(seeds[1], (3, 3, 3, C_LAT, C1), (27 * C_LAT) ** -0.5, 0.3125)
    weight_mid = gaussian(seeds[2], (3, 3, 3, C1, C1), (27 * C1) ** -0.5, 0.0625)
    weight_up = gaussian(seeds[3], (3, 3, 3, C1, C2), (27 * C1) ** -0.5, 0.0625)
    reward_grad = gaussian(seeds[4], (F, 2 * H, 2 * W, C2), 1.0, 6.0, ((0, 2), (1, 64), (3, 2)))
    return dict(latents=latents, weight_in=weight_in, weight_mid=weight_mid, weight_up=weight_up, reward_grad=reward_grad)


EPSILON = 1e-06

def conv_taps(padded, weight, backward):
    frames = padded.shape[0] - 2
    row_count = padded.shape[1] - 2
    col_count = padded.shape[2] - 2
    width_in = padded.shape[3]
    width_out = weight.shape[3] if backward else weight.shape[4]
    running = jnp.zeros((frames * row_count * col_count, width_out), jnp.float32)
    for tap_t in range(3):
        for tap_r in range(3):
            for tap_c in range(3):
                window_piece = padded[tap_t:tap_t + frames, tap_r:tap_r + row_count, tap_c:tap_c + col_count].reshape(-1, width_in)
                if backward:
                    kernel = weight[2 - tap_t, 2 - tap_r, 2 - tap_c]
                    running = running + lax.dot_general(window_piece, kernel, (((1,), (1,)), ((), ())), preferred_element_type=jnp.float32)
                else:
                    running = running + jnp.dot(window_piece, weight[tap_t, tap_r, tap_c], preferred_element_type=jnp.float32)
    return running.reshape(frames, row_count, col_count, width_out)

def conv_full(field, weight, backward):
    if backward:
        padded = jnp.pad(field, ((0, 2), (1, 1), (1, 1), (0, 0)))
    else:
        padded = jnp.pad(field, ((2, 0), (1, 1), (1, 1), (0, 0)))
    return conv_taps(padded, weight, backward)

def normalize(activation):
    inv_scale = lax.rsqrt(lax.optimization_barrier(jnp.mean(activation * activation, axis=3, keepdims=True)) + EPSILON)
    normed = activation * inv_scale
    return (normed, inv_scale, jax.nn.silu(normed).astype(jnp.bfloat16))

def norm_back(grad_h, normed, inv_scale):
    sigmoid_n = jax.nn.sigmoid(normed)
    grad_n = grad_h * sigmoid_n * (1.0 + normed * (1.0 - sigmoid_n))
    inner_mean = lax.optimization_barrier(jnp.mean(grad_n * normed, axis=3, keepdims=True))
    return inv_scale * (grad_n - normed * inner_mean)

def pool_blocks(field):
    frames, row_count, col_count, width = field.shape
    return field.reshape(frames, row_count // 2, 2, col_count // 2, 2, width).sum(axis=(2, 4))

def reference(latents, weight_in, weight_mid, weight_up, reward_grad):
    segment_one = conv_full(latents, weight_in, False)
    normed_one, scale_one, hidden_one = normalize(segment_one)
    segment_two = segment_one + conv_full(hidden_one, weight_mid, False)
    normed_two, scale_two, hidden_two = normalize(segment_two)
    lifted = jnp.repeat(jnp.repeat(hidden_two, 2, axis=1), 2, axis=2)
    decoded = conv_full(lifted, weight_up, False).astype(jnp.bfloat16)
    grad_up = pool_blocks(conv_full(reward_grad, weight_up, True))
    grad_two = norm_back(grad_up, normed_two, scale_two)
    grad_mid = conv_full(grad_two.astype(jnp.bfloat16), weight_mid, True)
    grad_one = grad_two + norm_back(grad_mid, normed_one, scale_one)
    latent_grad = conv_full(grad_one.astype(jnp.bfloat16), weight_in, True)
    return (decoded, latent_grad)
```

```python
import functools

import jax
import jax.numpy as jnp
from jax import lax
from jax.experimental import pallas as pl
from jax.experimental.pallas import tpu as pltpu
from jax.sharding import PartitionSpec as P

EPSILON = 1e-06
MESH = pl.DeviceIdType.MESH
BF = jnp.bfloat16
F32 = jnp.float32
NT = (((1,), (1,)), ((), ()))


def shift_rows(x, step, col, width):
    rolled = pltpu.roll(x, step % x.shape[0], axis=0)
    if step > 0:
        return jnp.where(col < step, 0.0, rolled)
    return jnp.where(col >= width + step, 0.0, rolled)


def kernel(n, lat_in, rew_in, win_hbm, wm_hbm, wu_hbm, dec_out, lg_out,
           wm, wu, win, w1, wz, par, gb, view, lat, lx, xc, h2, g2, sc, seg, n1, s1, n2, s2, acc, zs, zr, up, inter,
           wsem, xs_s, xs_r, rs_s, rs_r, la_s, la_r, hs_s, hs_r, gs_s, gs_r, zsem):
    s = lax.axis_index("sec")
    l = lax.axis_index("slab")
    c = lax.axis_index("ch")
    nxt = lax.rem(l + 1, n)
    prv = lax.rem(l + n - 1, n)
    rows = 4 * n
    c1 = wm.shape[3]

    copies = [
        pltpu.make_async_copy(win_hbm, win, wsem.at[0]),
        pltpu.make_async_copy(wm_hbm, wm, wsem.at[1]),
        pltpu.make_async_copy(wu_hbm, wu, wsem.at[2]),
    ]
    for copy in copies:
        copy.start()

    def remote(src, dst, ss, rs, dev):
        return pltpu.make_async_remote_copy(src_ref=src, dst_ref=dst, send_sem=ss, recv_sem=rs, device_id=dev, device_id_type=MESH)

    lane = lax.broadcasted_iota(jnp.int32, (n, 128), 1)
    row = lax.broadcasted_iota(jnp.int32, (n, 128), 0)
    for f in range(2):
        x = lat_in[f].astype(F32)
        total = jnp.zeros((n, 128), F32)
        for r in range(5):
            moved = shift_rows(x, 2 - r, row, n) if r != 2 else x
            if r:
                moved = pltpu.roll(moved, 16 * r, axis=1)
            total = total + moved
        view[f] = total.reshape(n, 1, 128)

    for i in range(2):
        lat[2 * s + i, l] = view[i, l]
    other = remote(view.at[:, l], lat.at[pl.ds(2 * s, 2), l], la_s.at[1], la_r.at[1], (1 - s, l, c))
    other.start()

    def send_lat(i, carry):
        to = lax.rem(l + i, n)
        remote(view.at[:, to], lat.at[pl.ds(2 * s, 2), l], la_s.at[0], la_r.at[0], (s, to, c)).start()
        remote(view.at[:, to], lat.at[pl.ds(2 * s, 2), l], la_s.at[1], la_r.at[1], (1 - s, to, c)).start()
        return carry

    lax.fori_loop(1, n, send_lat, 0)

    for f in range(2):
        for r in range(2):
            par[0] = rew_in[f, r].astype(F32)
            for p in range(2):
                gb[1 + r, c, 2 * s + f, p] = par[0, pl.ds(p, n, stride=2), :].astype(BF)
    peers = [(1 - s, c), (s, 1 - c), (1 - s, 1 - c)]
    x_copies = []
    for k, (ps, pc) in enumerate(peers):
        mine = gb.at[pl.ds(1, 2), c, pl.ds(2 * s, 2)]
        x_copies.append(remote(mine, mine, xs_s.at[k], xs_r.at[k], (ps, l, pc)))
        x_copies[-1].start()

    w1[...] = jnp.zeros_like(w1)
    wz[...] = jnp.zeros_like(wz)
    xc[...] = jnp.zeros_like(xc)
    lx[...] = jnp.zeros_like(lx)
    h2[...] = jnp.zeros_like(h2)
    sc[...] = jnp.zeros_like(sc)
    copies[0].wait()
    for a in range(3):
        for b in range(3):
            for e in range(3):
                piece = win[a, b, e]
                for rr in range(3):
                    w1[pl.ds((a * 3 + e) * 128 + 16 * (rr + b), 16), pl.ds(rr * c1, c1)] = piece
                for t in range(2):
                    j = t + 2 - a
                    wz[j, e, pl.ds(b * 32 + t * 16, 16), :] = piece

    for copy in x_copies:
        copy.wait_recv()
    r_copies = [
        remote(gb.at[2], gb.at[0], rs_s.at[0], rs_r.at[0], (s, nxt, c)),
        remote(gb.at[1], gb.at[3], rs_s.at[1], rs_r.at[1], (s, prv, c)),
    ]
    for copy in r_copies:
        copy.start()

    def wait_bytes(ref, sem):
        pltpu.make_async_copy(ref, ref, sem).wait()

    wait_bytes(lat.at[pl.ds(0, 2), pl.ds(0, n - 1)], la_r.at[0])
    wait_bytes(lat.at[pl.ds(0, 2)], la_r.at[1])

    for f in range(4):
        x = lat[f].reshape(n, 128)
        for e in range(3):
            moved = (shift_rows(x, 1 - e, row, n) if e != 1 else x).astype(BF)
            for a in range(3):
                t = f + 2 - a
                if t < 4:
                    lx[t, :, pl.ds((a * 3 + e) * 128, 128)] = moved
    big_col = lax.rem(lax.broadcasted_iota(jnp.int32, (rows, c1), 0), n)

    def spread(value, target, r, first, flip):
        for e in range(3):
            step = (e - 1) if flip else (1 - e)
            moved = shift_rows(value, step, big_col, n) if e != 1 else value
            target[r, pl.ds(first, 4), :, pl.ds(e * c1, c1)] = moved.astype(BF).reshape(4, n, c1)

    def norm(v):
        inv = lax.rsqrt(jnp.sum(v * v, axis=1, keepdims=True) / c1 + EPSILON)
        normed = v * inv
        return normed, inv, normed * jax.nn.sigmoid(normed)

    def norm_back(dh, normed, inv):
        sig = jax.nn.sigmoid(normed)
        dn = dh * sig * (1.0 + normed * (1.0 - sig))
        mean = jnp.sum(dn * normed, axis=1, keepdims=True) / c1
        return inv * (dn - normed * mean)

    low_ok = l > 0
    high_ok = l < n - 1
    for rr in range(3):
        seg[...] = jnp.dot(lx[...].reshape(rows, 1152), w1[:, rr * c1:(rr + 1) * c1], preferred_element_type=F32)
        normed, inv, hidden = norm(seg[...])
        if rr == 0:
            hidden = jnp.where(low_ok, hidden, 0.0)
        if rr == 2:
            hidden = jnp.where(high_ok, hidden, 0.0)
        spread(hidden, xc, rr, 2, False)
        if rr == 1:
            n1[...] = normed
            s1[...] = inv
            acc[...] = seg[...]

    copies[1].wait()

    def mid_tap(i, carry):
        a = i // 3
        b = i % 3
        left = xc[b, pl.ds(a, 4)].reshape(rows, 3 * c1)
        acc[...] += jnp.dot(left, wm[a, b].reshape(3 * c1, c1), preferred_element_type=F32)
        return carry

    lax.fori_loop(0, 9, mid_tap, 0)
    normed, inv, hidden = norm(acc[...])
    n2[...] = normed
    s2[...] = inv
    h2[1, pl.ds(2, 4)] = hidden.astype(BF).reshape(4, n, c1)
    mine = h2.at[1, pl.ds(2, 4)]
    h_copies = [
        remote(mine, h2.at[0, pl.ds(2, 4)], hs_s.at[0], hs_r.at[0], (s, nxt, c)),
        remote(mine, h2.at[2, pl.ds(2, 4)], hs_s.at[1], hs_r.at[1], (s, prv, c)),
    ]

    copies[2].wait()
    for copy in r_copies:
        copy.wait_recv()
    col64 = lax.broadcasted_iota(jnp.int32, (n, 96), 0)
    for f in range(4):
        for b in range(3):
            for half in range(2):
                first = gb[2 - b, half, f].astype(F32)
                second = gb[3 - b, half, f].astype(F32)
                if b == 2:
                    first = jnp.where(low_ok, first, 0.0)
                if b == 0:
                    second = jnp.where(high_ok, second, 0.0)
                both = first + second
                even, odd = both[0], both[1]
                whole = even + odd
                cross = odd + shift_rows(even, -1, col64, n)
                back = shift_rows(odd, 1, col64, n) + even
                for e, value in ((0, cross), (1, whole), (2, back)):
                    sc[b, e, f, :, pl.ds(half * 96, 96)] = value.astype(BF)
    up[...] = jnp.zeros_like(up)

    def up_tap(i, carry):
        a = i // 3
        b = i % 3
        for e in range(3):
            left = sc[b, e, pl.ds(2 - a, 4)].reshape(rows, 192)
            up[...] += lax.dot_general(left, wu[a, b, e], NT, preferred_element_type=F32)
        return carry

    lax.fori_loop(0, 9, up_tap, 0)
    grad_two = norm_back(up[...], n2[...], s2[...])
    up[...] = grad_two
    g2[1] = grad_two.astype(BF).reshape(4, n, c1)
    g_copies = [
        remote(g2.at[1], g2.at[0], gs_s.at[0], gs_r.at[0], (s, nxt, c)),
        remote(g2.at[1], g2.at[2], gs_s.at[1], gs_r.at[1], (s, prv, c)),
    ]
    for copy in g_copies:
        copy.start()
    for copy in h_copies:
        copy.start()

    zero_pad = jnp.zeros((2, n, 3 * c1), BF)
    for rr in range(3):
        xc[rr, pl.ds(4, 2)] = zero_pad
    spread(grad_two.astype(BF).astype(F32), xc, 1, 0, True)
    acc[...] = jnp.zeros_like(acc)

    def back_tap(a, b):
        for e in range(3):
            left = xc[2 - b, pl.ds(2 - a, 4), :, pl.ds(e * c1, c1)].reshape(rows, c1)
            acc[...] += lax.dot_general(left, wm[a, b, e], NT, preferred_element_type=F32)

    def own_tap(a, carry):
        back_tap(a, 1)
        return carry

    lax.fori_loop(0, 3, own_tap, 0)
    for copy in g_copies:
        copy.wait_recv()
    for rr, ok in ((0, low_ok), (2, high_ok)):
        halo = g2[rr].reshape(rows, c1).astype(F32)
        spread(jnp.where(ok, halo, 0.0), xc, rr, 0, True)

    def halo_tap(i, carry):
        back_tap(i // 2, (i % 2) * 2)
        return carry

    lax.fori_loop(0, 6, halo_tap, 0)
    grad_one = up[...] + norm_back(acc[...], n1[...], s1[...])
    spread(grad_one.astype(BF).astype(F32), xc, 1, 0, True)
    total = jnp.zeros((n, 128), F32)
    for j in range(4):
        for e in range(3):
            left = xc[1, 2 * s + j, :, pl.ds(e * c1, c1)]
            total = total + lax.dot_general(left, wz[j, e], NT, preferred_element_type=F32)
    zs[...] = total.reshape(n, 1, 128)
    zr[l] = zs[l]

    def send_z(i, carry):
        to = lax.rem(l + i, n)
        remote(zs.at[to], zr.at[l], zsem.at[0], zsem.at[1], (s, to, c)).start()
        return carry

    lax.fori_loop(1, n, send_z, 0)

    for copy in h_copies:
        copy.wait_recv()
    for rr, edge in ((0, l == 0), (2, l == n - 1)):

        @pl.when(edge)
        def _():
            h2[rr] = jnp.zeros_like(h2[rr])

    inter[...] = jnp.zeros_like(inter)
    col128 = lax.rem(lax.broadcasted_iota(jnp.int32, (2 * n, 192), 0), n)

    def dec_tap(a, carry):
        two = pl.ds(2 * s + a, 2)
        for e in range(3):
            inter[e, pl.ds(0, rows)] += jnp.dot(h2[0:2, two].reshape(rows, c1), wu[a, 0, e], preferred_element_type=F32)
            inter[e, pl.ds(0, rows)] += jnp.dot(h2[1:3, two].reshape(rows, c1), wu[a, 2, e], preferred_element_type=F32)
            inter[e, pl.ds(rows, 2 * n)] += jnp.dot(h2[1, two].reshape(2 * n, c1), wu[a, 1, e], preferred_element_type=F32)
        return carry

    lax.fori_loop(0, 3, dec_tap, 0)
    for dy in range(2):
        by_tap = [inter[e, pl.ds(dy * 2 * n, 2 * n)] + inter[e, pl.ds(rows, 2 * n)] for e in range(3)]
        for dx in range(2):
            if dx == 0:
                full = shift_rows(by_tap[0], 1, col128, n) + by_tap[1] + by_tap[2]
            else:
                full = by_tap[0] + by_tap[1] + shift_rows(by_tap[2], -1, col128, n)
            half = jnp.where(c == 0, full[:, :96], full[:, 96:])
            for f in range(2):
                par[f, pl.ds(dx, n, stride=2), :] = half[f * n:(f + 1) * n]
        for f in range(2):
            dec_out[f, dy] = par[f].astype(BF)

    wait_bytes(zr.at[pl.ds(0, n - 1)], zsem.at[1])
    z = zr[...].reshape(n, 128)
    result = shift_rows(z, -1, row, n) + pltpu.roll(z, 128 - 32, axis=1) + pltpu.roll(shift_rows(z, 1, row, n), 128 - 64, axis=1)
    lg_out[...] = result

    wait_bytes(view.at[:, pl.ds(0, n - 1)], la_s.at[0])
    wait_bytes(view, la_s.at[1])
    wait_bytes(zs.at[pl.ds(0, n - 1)], zsem.at[0])
    for copy in x_copies + r_copies + h_copies + g_copies:
        copy.wait_send()


def shards(n, latents, weight_in, weight_mid, weight_up, reward_grad):
    c1 = weight_mid.shape[4]
    c2 = weight_up.shape[4]
    rows = 4 * n
    lat16 = jnp.pad(latents.reshape(2, n, 16), ((0, 0), (0, 0), (0, 112)))
    vm = pltpu.VMEM
    dma = pltpu.SemaphoreType.DMA
    any_spec = pl.BlockSpec(memory_space=pl.ANY)
    vm_spec = pl.BlockSpec(memory_space=vm)
    decoded, grad = pl.pallas_call(
        functools.partial(kernel, n),
        out_shape=(
            jax.ShapeDtypeStruct((2, 2, 2 * n, c2 // 2), BF),
            jax.ShapeDtypeStruct((n, 128), F32),
        ),
        in_specs=[vm_spec, vm_spec, any_spec, any_spec, any_spec],
        out_specs=(vm_spec, vm_spec),
        scratch_shapes=[
            vm((3, 3, 3, c1, c1), BF),
            vm((3, 3, 3, c1, c2), BF),
            vm((3, 3, 3, 16, c1), BF),
            vm((1152, 3 * c1), BF),
            vm((4, 3, 128, c1), BF),
            vm((2, 2 * n, c2 // 2), F32),
            vm((4, 2, 4, 2, n, c2 // 2), BF),
            vm((2, n, 1, 128), F32),
            vm((4, n, 1, 128), F32),
            vm((4, n, 1152), BF),
            vm((3, 6, n, 3 * c1), BF),
            vm((3, 6, n, c1), BF),
            vm((3, 4, n, c1), BF),
            vm((3, 3, 6, n, c2), BF),
            vm((rows, c1), F32),
            vm((rows, c1), F32),
            vm((rows, 1), F32),
            vm((rows, c1), F32),
            vm((rows, 1), F32),
            vm((rows, c1), F32),
            vm((n, 1, 128), F32),
            vm((n, 1, 128), F32),
            vm((rows, c1), F32),
            vm((3, 6 * n, c2), F32),
            dma((3,)), dma((3,)), dma((3,)), dma((2,)), dma((2,)), dma((2,)), dma((2,)),
            dma((2,)), dma((2,)), dma((2,)), dma((2,)), dma((2,)),
        ],
        compiler_params=pltpu.CompilerParams(has_side_effects=True, vmem_limit_bytes=60 * 1024 * 1024),
    )(lat16, reward_grad, weight_in, weight_mid, weight_up)
    latent_grad = grad[:, :32].reshape(n, 2, 16).transpose(1, 0, 2).reshape(2, n, 1, 16)
    return decoded, latent_grad


def solution(mesh):
    return jax.shard_map(
        functools.partial(shards, mesh.shape["slab"]),
        mesh=mesh,
        in_specs=(P("sec", None, "slab", None), P(), P(), P(), P("sec", "slab", None, "ch")),
        out_specs=(P("sec", "slab", None, "ch"), P("sec", None, "slab", None)),
        check_vma=False,
    )
```

```python
import functools

import jax
import jax.numpy as jnp
from jax import lax
from jax.experimental import pallas as pl
from jax.experimental.pallas import tpu as pltpu
from jax.sharding import PartitionSpec as P

EPSILON = 1e-06
MESH = pl.DeviceIdType.MESH
BF = jnp.bfloat16
F32 = jnp.float32
NT = (((1,), (1,)), ((), ()))


def shift_rows(x, step, col, width):
    rolled = pltpu.roll(x, step % x.shape[0], axis=0)
    if step > 0:
        return jnp.where(col < step, 0.0, rolled)
    return jnp.where(col >= width + step, 0.0, rolled)


def kernel(n, lat_in, rew_hbm, win_hbm, wm_hbm, wu_hbm, dec_out, lg_out,
           wm, wu, win, w1, wz, bsel, par, gb, view, lat, lx, xc, h2, g2, sc, seg, n1, s1, n2, s2, acc, zs, zr, up, inter,
           wsem, own_sem, xs_s, xs_r, rs_s, rs_r, la_s, la_r, hs_s, hs_r, gs_s, gs_r, zsem):
    s = lax.axis_index("sec")
    l = lax.axis_index("slab")
    c = lax.axis_index("ch")
    nxt = lax.rem(l + 1, n)
    prv = lax.rem(l + n - 1, n)
    rows = 4 * n
    c1 = wm.shape[3]
    c2 = wu.shape[3]

    copies = [
        pltpu.make_async_copy(win_hbm, win, wsem.at[0]),
        pltpu.make_async_copy(wm_hbm, wm, wsem.at[1]),
        pltpu.make_async_copy(wu_hbm, wu, wsem.at[2]),
    ]
    own = pltpu.make_async_copy(rew_hbm, gb.at[pl.ds(2 * s, 2), pl.ds(1, 2), c], own_sem)
    for copy in copies[:1] + [own] + copies[1:]:
        copy.start()

    barrier = pltpu.get_barrier_semaphore()

    def greet(ps, to, pc):
        pl.semaphore_signal(barrier, inc=1, device_id=(ps, to, pc), device_id_type=MESH)

    def greet_all(i, carry):
        to = lax.rem(l + i, n)
        greet(s, to, c)
        greet(1 - s, to, c)
        return carry

    peers = [(1 - s, c), (s, 1 - c), (1 - s, 1 - c)]
    for ps, pc in peers:
        greet(ps, l, pc)
    lax.fori_loop(1, n, greet_all, 0)

    def remote(src, dst, ss, rs, dev):
        return pltpu.make_async_remote_copy(src_ref=src, dst_ref=dst, send_sem=ss, recv_sem=rs, device_id=dev, device_id_type=MESH)

    row = lax.broadcasted_iota(jnp.int32, (n, 128), 0)
    for f in range(2):
        x = jnp.concatenate([lat_in[f].astype(F32), jnp.zeros((16, 128 - n), F32)], axis=1)
        stack = [pltpu.roll(x, (2 - r) % 128, axis=1) if r != 2 else x for r in range(5)]
        both = jnp.concatenate(stack + [jnp.zeros((48, 128), F32)], axis=0)
        view[f] = both.T[:n].reshape(n, 1, 128)

    pick_row = lax.broadcasted_iota(jnp.int32, (n, 2 * n), 0)
    pick_col = lax.broadcasted_iota(jnp.int32, (n, 2 * n), 1)
    for e in range(3):
        delta = pick_col - 2 * pick_row - (1 - e)
        bsel[pl.ds(e * n, n)] = jnp.where((delta == 0) | (delta == 1), 1.0, 0.0).astype(BF)
    w1[...] = jnp.zeros_like(w1)
    wz[...] = jnp.zeros_like(wz)
    xc[:, pl.ds(0, 2)] = jnp.zeros((3, 2, n, 3 * c1), BF)
    lx[...] = jnp.zeros_like(lx)
    h2[:, pl.ds(0, 2)] = jnp.zeros((3, 2, n, c1), BF)
    sc[:, :, pl.ds(4, 2)] = jnp.zeros((3, 3, 2, n, c2), BF)
    copies[0].wait()
    for a in range(3):
        for b in range(3):
            for e in range(3):
                piece = win[a, b, e]
                for rr in range(3):
                    w1[pl.ds((a * 3 + e) * 128 + 16 * (rr + b), 16), pl.ds(rr * c1, c1)] = piece
                for t in range(2):
                    j = t + 2 - a
                    wz[j, e, pl.ds(b * 32 + t * 16, 16), :] = piece
    for i in range(2):
        lat[2 * s + i, l] = view[i, l]

    pl.semaphore_wait(barrier, 2 * n + 1)

    def wait_bytes(ref, sem):
        pltpu.make_async_copy(ref, ref, sem).wait()

    other = remote(view.at[:, l], lat.at[pl.ds(2 * s, 2), l], la_s.at[1], la_r.at[1], (1 - s, l, c))
    other.start()

    def send_lat(i, carry):
        to = lax.rem(l + i, n)
        remote(view.at[:, to], lat.at[pl.ds(2 * s, 2), l], la_s.at[0], la_r.at[0], (s, to, c)).start()
        remote(view.at[:, to], lat.at[pl.ds(2 * s, 2), l], la_s.at[1], la_r.at[1], (1 - s, to, c)).start()
        return carry

    lax.fori_loop(1, n, send_lat, 0)
    x_copies = []
    for k, (ps, pc) in enumerate(peers):
        x_copies.append(remote(rew_hbm, gb.at[pl.ds(2 * s, 2), pl.ds(1, 2), c], xs_s.at[k], xs_r.at[k], (ps, l, pc)))
        x_copies[-1].start()

    wait_bytes(lat.at[pl.ds(0, 2), pl.ds(0, n - 1)], la_r.at[0])
    wait_bytes(lat.at[pl.ds(0, 2)], la_r.at[1])

    for f in range(4):
        x = lat[f].reshape(n, 128)
        for e in range(3):
            moved = (shift_rows(x, 1 - e, row, n) if e != 1 else x).astype(BF)
            for a in range(3):
                t = f + 2 - a
                if t < 4:
                    lx[t, :, pl.ds((a * 3 + e) * 128, 128)] = moved
    big_col = lax.rem(lax.broadcasted_iota(jnp.int32, (rows, c1), 0), n)

    def spread(value, target, r, first, flip):
        for e in range(3):
            step = (e - 1) if flip else (1 - e)
            moved = shift_rows(value, step, big_col, n) if e != 1 else value
            target[r, pl.ds(first, 4), :, pl.ds(e * c1, c1)] = moved.astype(BF).reshape(4, n, c1)

    def norm(v):
        inv = lax.rsqrt(jnp.sum(v * v, axis=1, keepdims=True) / c1 + EPSILON)
        normed = v * inv
        return normed, inv, normed * jax.nn.sigmoid(normed)

    def norm_back(dh, normed, inv):
        sig = jax.nn.sigmoid(normed)
        dn = dh * sig * (1.0 + normed * (1.0 - sig))
        mean = jnp.sum(dn * normed, axis=1, keepdims=True) / c1
        return inv * (dn - normed * mean)

    low_ok = l > 0
    high_ok = l < n - 1
    for rr in range(3):
        seg[...] = jnp.dot(lx[...].reshape(rows, 1152), w1[:, rr * c1:(rr + 1) * c1], preferred_element_type=F32)
        normed, inv, hidden = norm(seg[...])
        if rr == 0:
            hidden = jnp.where(low_ok, hidden, 0.0)
        if rr == 2:
            hidden = jnp.where(high_ok, hidden, 0.0)
        spread(hidden, xc, rr, 2, False)
        if rr == 1:
            n1[...] = normed
            s1[...] = inv
            acc[...] = seg[...]

    own.wait()
    for copy in x_copies:
        copy.wait_recv()
    r_copies = [
        remote(gb.at[:, 2], gb.at[:, 0], rs_s.at[0], rs_r.at[0], (s, nxt, c)),
        remote(gb.at[:, 1], gb.at[:, 3], rs_s.at[1], rs_r.at[1], (s, prv, c)),
    ]
    for copy in r_copies:
        copy.start()

    copies[1].wait()

    def mid_tap(i, carry):
        a = i // 3
        b = i % 3
        left = xc[b, pl.ds(a, 4)].reshape(rows, 3 * c1)
        acc[...] += jnp.dot(left, wm[a, b].reshape(3 * c1, c1), preferred_element_type=F32)
        return carry

    lax.fori_loop(0, 9, mid_tap, 0)
    normed, inv, hidden = norm(acc[...])
    n2[...] = normed
    s2[...] = inv
    h2[1, pl.ds(2, 4)] = hidden.astype(BF).reshape(4, n, c1)
    mine = h2.at[1, pl.ds(2, 4)]
    h_copies = [
        remote(mine, h2.at[0, pl.ds(2, 4)], hs_s.at[0], hs_r.at[0], (s, nxt, c)),
        remote(mine, h2.at[2, pl.ds(2, 4)], hs_s.at[1], hs_r.at[1], (s, prv, c)),
    ]
    for copy in h_copies:
        copy.start()

    copies[2].wait()
    for copy in r_copies:
        copy.wait_recv()
    for i, edge in ((0, l == 0), (3, l == n - 1)):

        @pl.when(edge)
        def _():
            gb[:, i] = jnp.zeros_like(gb[:, i])

    for f in range(4):
        for b in range(3):
            first = lax.dot_general(bsel[...], gb[f, 2 - b].reshape(c2, 2 * n), NT, preferred_element_type=F32)
            second = lax.dot_general(bsel[...], gb[f, 3 - b].reshape(c2, 2 * n), NT, preferred_element_type=F32)
            pooled = (first + second).astype(BF)
            for e in range(3):
                sc[b, e, f] = pooled[e * n:(e + 1) * n]
    up[...] = jnp.zeros_like(up)

    def up_tap(i, carry):
        a = i // 3
        b = i % 3
        for e in range(3):
            left = sc[b, e, pl.ds(2 - a, 4)].reshape(rows, c2)
            up[...] += jnp.dot(left, wu[a, b, e], preferred_element_type=F32)
        return carry

    lax.fori_loop(0, 9, up_tap, 0)
    grad_two = norm_back(up[...], n2[...], s2[...])
    up[...] = grad_two
    g2[1] = grad_two.astype(BF).reshape(4, n, c1)
    g_copies = [
        remote(g2.at[1], g2.at[0], gs_s.at[0], gs_r.at[0], (s, nxt, c)),
        remote(g2.at[1], g2.at[2], gs_s.at[1], gs_r.at[1], (s, prv, c)),
    ]
    for copy in g_copies:
        copy.start()

    zero_pad = jnp.zeros((2, n, 3 * c1), BF)
    for rr in range(3):
        xc[rr, pl.ds(4, 2)] = zero_pad
    spread(grad_two.astype(BF).astype(F32), xc, 1, 0, True)
    acc[...] = jnp.zeros_like(acc)

    def back_tap(a, b):
        for e in range(3):
            left = xc[2 - b, pl.ds(2 - a, 4), :, pl.ds(e * c1, c1)].reshape(rows, c1)
            acc[...] += lax.dot_general(left, wm[a, b, e], NT, preferred_element_type=F32)

    def own_tap(a, carry):
        back_tap(a, 1)
        return carry

    lax.fori_loop(0, 3, own_tap, 0)
    for copy in g_copies:
        copy.wait_recv()
    for rr, ok in ((0, low_ok), (2, high_ok)):
        halo = g2[rr].reshape(rows, c1).astype(F32)
        spread(jnp.where(ok, halo, 0.0), xc, rr, 0, True)

    def halo_tap(i, carry):
        back_tap(i // 2, (i % 2) * 2)
        return carry

    lax.fori_loop(0, 6, halo_tap, 0)
    grad_one = up[...] + norm_back(acc[...], n1[...], s1[...])
    spread(grad_one.astype(BF).astype(F32), xc, 1, 0, True)
    total = jnp.zeros((n, 128), F32)
    for j in range(4):
        for e in range(3):
            left = xc[1, 2 * s + j, :, pl.ds(e * c1, c1)]
            total = total + lax.dot_general(left, wz[j, e], NT, preferred_element_type=F32)
    zs[...] = total.reshape(n, 1, 128)
    zr[l] = zs[l]

    def send_z(i, carry):
        to = lax.rem(l + i, n)
        remote(zs.at[to], zr.at[l], zsem.at[0], zsem.at[1], (s, to, c)).start()
        return carry

    lax.fori_loop(1, n, send_z, 0)

    for copy in h_copies:
        copy.wait_recv()
    for rr, edge in ((0, l == 0), (2, l == n - 1)):

        @pl.when(edge)
        def _():
            h2[rr] = jnp.zeros_like(h2[rr])

    inter[...] = jnp.zeros_like(inter)
    col128 = lax.rem(lax.broadcasted_iota(jnp.int32, (2 * n, c2 // 2), 0), n)

    def dec_tap(a, carry):
        two = pl.ds(2 * s + a, 2)
        half = pl.ds(c * (c2 // 2), c2 // 2)
        for e in range(3):
            inter[e, pl.ds(0, rows)] += lax.dot_general(h2[0:2, two].reshape(rows, c1), wu[a, 0, e, half], NT, preferred_element_type=F32)
            inter[e, pl.ds(0, rows)] += lax.dot_general(h2[1:3, two].reshape(rows, c1), wu[a, 2, e, half], NT, preferred_element_type=F32)
            inter[e, pl.ds(rows, 2 * n)] += lax.dot_general(h2[1, two].reshape(2 * n, c1), wu[a, 1, e, half], NT, preferred_element_type=F32)
        return carry

    lax.fori_loop(0, 3, dec_tap, 0)
    for dy in range(2):
        by_tap = [inter[e, pl.ds(dy * 2 * n, 2 * n)] + inter[e, pl.ds(rows, 2 * n)] for e in range(3)]
        for dx in range(2):
            if dx == 0:
                full = shift_rows(by_tap[0], 1, col128, n) + by_tap[1] + by_tap[2]
            else:
                full = by_tap[0] + by_tap[1] + shift_rows(by_tap[2], -1, col128, n)
            for f in range(2):
                par[f, pl.ds(dx, n, stride=2), :] = full[f * n:(f + 1) * n]
        for f in range(2):
            dec_out[f, dy] = par[f].T.astype(BF)

    wait_bytes(zr.at[pl.ds(0, n - 1)], zsem.at[1])
    z = zr[...].reshape(n, 128)
    result = shift_rows(z, -1, row, n) + pltpu.roll(z, 128 - 32, axis=1) + pltpu.roll(shift_rows(z, 1, row, n), 128 - 64, axis=1)
    lg_out[...] = result.T[:32].reshape(2, 16, n)

    wait_bytes(view.at[:, pl.ds(0, n - 1)], la_s.at[0])
    wait_bytes(view, la_s.at[1])
    wait_bytes(zs.at[pl.ds(0, n - 1)], zsem.at[0])
    for copy in x_copies + r_copies + h_copies + g_copies:
        copy.wait_send()


def shards(n, latents, weight_in, weight_mid, weight_up, reward_grad):
    c1 = weight_mid.shape[4]
    c2 = weight_up.shape[4]
    rows = 4 * n
    vm = pltpu.VMEM
    dma = pltpu.SemaphoreType.DMA
    any_spec = pl.BlockSpec(memory_space=pl.ANY)
    vm_spec = pl.BlockSpec(memory_space=vm)
    decoded, grad = pl.pallas_call(
        functools.partial(kernel, n),
        out_shape=(
            jax.ShapeDtypeStruct((2, 2, c2 // 2, 2 * n), BF),
            jax.ShapeDtypeStruct((2, 16, n), F32),
        ),
        in_specs=[vm_spec, any_spec, any_spec, any_spec, any_spec],
        out_specs=(vm_spec, vm_spec),
        scratch_shapes=[
            vm((3, 3, 3, c1, c1), BF),
            vm((3, 3, 3, c2, c1), BF),
            vm((3, 3, 3, 16, c1), BF),
            vm((1152, 3 * c1), BF),
            vm((4, 3, 128, c1), BF),
            vm((3 * n, 2 * n), BF),
            vm((2, 2 * n, c2 // 2), F32),
            vm((4, 4, 2, c2 // 2, 2 * n), BF),
            vm((2, n, 1, 128), F32),
            vm((4, n, 1, 128), F32),
            vm((4, n, 1152), BF),
            vm((3, 6, n, 3 * c1), BF),
            vm((3, 6, n, c1), BF),
            vm((3, 4, n, c1), BF),
            vm((3, 3, 6, n, c2), BF),
            vm((rows, c1), F32),
            vm((rows, c1), F32),
            vm((rows, 1), F32),
            vm((rows, c1), F32),
            vm((rows, 1), F32),
            vm((rows, c1), F32),
            vm((n, 1, 128), F32),
            vm((n, 1, 128), F32),
            vm((rows, c1), F32),
            vm((3, 6 * n, c2 // 2), F32),
            dma((3,)), dma, dma((3,)), dma((3,)), dma((2,)), dma((2,)), dma((2,)), dma((2,)),
            dma((2,)), dma((2,)), dma((2,)), dma((2,)), dma((2,)),
        ],
        compiler_params=pltpu.CompilerParams(has_side_effects=True, collective_id=0, vmem_limit_bytes=60 * 1024 * 1024),
    )(latents.reshape(2, n, 16).transpose(0, 2, 1), reward_grad.transpose(0, 1, 3, 2), weight_in, weight_mid, weight_up.transpose(0, 1, 2, 4, 3))
    return decoded.transpose(0, 1, 3, 2), grad.transpose(0, 2, 1).reshape(2, n, 1, 16)


def solution(mesh):
    return jax.shard_map(
        functools.partial(shards, mesh.shape["slab"]),
        mesh=mesh,
        in_specs=(P("sec", None, "slab", None), P(), P(), P(), P("sec", "slab", None, "ch")),
        out_specs=(P("sec", "slab", None, "ch"), P("sec", None, "slab", None)),
        check_vma=False,
    )
```

```python
import functools

import jax
import jax.numpy as jnp
from jax import lax
from jax.experimental import pallas as pl
from jax.experimental.pallas import tpu as pltpu
from jax.sharding import PartitionSpec as P

EPSILON = 1e-06
MESH = pl.DeviceIdType.MESH
BF = jnp.bfloat16
F32 = jnp.float32
NT = (((1,), (1,)), ((), ()))


def shift_rows(x, step, col, width):
    rolled = pltpu.roll(x, step % x.shape[0], axis=0)
    if step > 0:
        return jnp.where(col < step, 0.0, rolled)
    return jnp.where(col >= width + step, 0.0, rolled)


def kernel(n, lat_in, rew_hbm, win_hbm, wm_hbm, wu_hbm, dec_out, lg_out,
           wm, wu, win, w1, wz, bsel, par, gb, view, lat, lx, xc, h2, g2, sc, seg, n1, s1, n2, s2, acc, zs, zr, up, inter,
           wsem, own_sem, xs_s, xs_r, rs_s, rs_r, la_s, la_r, hs_s, hs_r, gs_s, gs_r, zsem):
    s = lax.axis_index("sec")
    l = lax.axis_index("slab")
    c = lax.axis_index("ch")
    nxt = lax.rem(l + 1, n)
    prv = lax.rem(l + n - 1, n)
    rows = 4 * n
    c1 = wm.shape[3]
    c2 = wu.shape[3]

    copies = [
        pltpu.make_async_copy(win_hbm, win, wsem.at[0]),
        pltpu.make_async_copy(wm_hbm, wm, wsem.at[1]),
        pltpu.make_async_copy(wu_hbm, wu, wsem.at[2]),
    ]
    own = pltpu.make_async_copy(rew_hbm, gb.at[pl.ds(2 * s, 2), pl.ds(1, 2), c], own_sem)
    for copy in copies[:1] + [own] + copies[1:]:
        copy.start()

    barrier = pltpu.get_barrier_semaphore()

    def greet(ps, to, pc):
        pl.semaphore_signal(barrier, inc=1, device_id=(ps, to, pc), device_id_type=MESH)

    chunk = 9 if (n - 1) % 9 == 0 else n - 1

    def each_partner(act):
        def step(k, carry):
            for i in range(chunk):
                act(lax.rem(l + k * chunk + (1 + i), n))
            return carry

        lax.fori_loop(0, (n - 1) // chunk, step, 0)

    def greet_all(to):
        greet(s, to, c)
        greet(1 - s, to, c)

    peers = [(1 - s, c), (s, 1 - c), (1 - s, 1 - c)]
    for ps, pc in peers:
        greet(ps, l, pc)
    each_partner(greet_all)

    def remote(src, dst, ss, rs, dev):
        return pltpu.make_async_remote_copy(src_ref=src, dst_ref=dst, send_sem=ss, recv_sem=rs, device_id=dev, device_id_type=MESH)

    row = lax.broadcasted_iota(jnp.int32, (n, 128), 0)
    for f in range(2):
        x = jnp.concatenate([lat_in[f].astype(F32), jnp.zeros((16, 128 - n), F32)], axis=1)
        stack = [pltpu.roll(x, (2 - r) % 128, axis=1) if r != 2 else x for r in range(5)]
        both = jnp.concatenate(stack + [jnp.zeros((48, 128), F32)], axis=0)
        view[f] = both.T[:n].reshape(n, 1, 128)

    pick_row = lax.broadcasted_iota(jnp.int32, (n, 2 * n), 0)
    pick_col = lax.broadcasted_iota(jnp.int32, (n, 2 * n), 1)
    for e in range(3):
        delta = pick_col - 2 * pick_row - (1 - e)
        bsel[pl.ds(e * n, n)] = jnp.where((delta == 0) | (delta == 1), 1.0, 0.0).astype(BF)
    w1[...] = jnp.zeros_like(w1)
    wz[...] = jnp.zeros_like(wz)
    xc[:, pl.ds(0, 2)] = jnp.zeros((3, 2, n, 3 * c1), BF)
    lx[...] = jnp.zeros_like(lx)
    h2[:, pl.ds(0, 2)] = jnp.zeros((3, 2, n, c1), BF)
    sc[:, :, pl.ds(4, 2)] = jnp.zeros((3, 3, 2, n, c2), BF)
    copies[0].wait()
    for a in range(3):
        for b in range(3):
            for e in range(3):
                piece = win[a, b, e]
                for rr in range(3):
                    w1[pl.ds((a * 3 + e) * 128 + 16 * (rr + b), 16), pl.ds(rr * c1, c1)] = piece
                for t in range(2):
                    j = t + 2 - a
                    wz[j, e, pl.ds(b * 32 + t * 16, 16), :] = piece
    for i in range(2):
        lat[2 * s + i, l] = view[i, l]

    pl.semaphore_wait(barrier, 2 * n + 1)

    def wait_bytes(ref, sem):
        pltpu.make_async_copy(ref, ref, sem).wait()

    x_copies = []
    for k, (ps, pc) in enumerate(peers):
        x_copies.append(remote(rew_hbm, gb.at[pl.ds(2 * s, 2), pl.ds(1, 2), c], xs_s.at[k], xs_r.at[k], (ps, l, pc)))
        x_copies[-1].start()

    def send_lat(to):
        remote(view.at[:, to], lat.at[pl.ds(2 * s, 2), l], la_s.at[0], la_r.at[0], (s, to, c)).start()
        remote(view.at[:, to], lat.at[pl.ds(2 * s, 2), l], la_s.at[1], la_r.at[1], (1 - s, to, c)).start()

    each_partner(send_lat)
    other = remote(view.at[:, l], lat.at[pl.ds(2 * s, 2), l], la_s.at[1], la_r.at[1], (1 - s, l, c))
    other.start()

    own.wait()
    for copy in x_copies:
        copy.wait_recv()
    r_copies = [
        remote(gb.at[:, 2], gb.at[:, 0], rs_s.at[0], rs_r.at[0], (s, nxt, c)),
        remote(gb.at[:, 1], gb.at[:, 3], rs_s.at[1], rs_r.at[1], (s, prv, c)),
    ]
    for copy in r_copies:
        copy.start()

    wait_bytes(lat.at[pl.ds(0, 2), pl.ds(0, n - 1)], la_r.at[0])
    wait_bytes(lat.at[pl.ds(0, 2)], la_r.at[1])

    for f in range(4):
        x = lat[f].reshape(n, 128)
        for e in range(3):
            moved = (shift_rows(x, 1 - e, row, n) if e != 1 else x).astype(BF)
            for a in range(3):
                t = f + 2 - a
                if t < 4:
                    lx[t, :, pl.ds((a * 3 + e) * 128, 128)] = moved
    big_col = lax.rem(lax.broadcasted_iota(jnp.int32, (rows, c1), 0), n)

    def spread(value, target, r, first, flip):
        for e in range(3):
            step = (e - 1) if flip else (1 - e)
            moved = shift_rows(value, step, big_col, n) if e != 1 else value
            target[r, pl.ds(first, 4), :, pl.ds(e * c1, c1)] = moved.astype(BF).reshape(4, n, c1)

    def norm(v):
        inv = lax.rsqrt(jnp.sum(v * v, axis=1, keepdims=True) / c1 + EPSILON)
        normed = v * inv
        return normed, inv, normed * jax.nn.sigmoid(normed)

    def norm_back(dh, normed, inv):
        sig = jax.nn.sigmoid(normed)
        dn = dh * sig * (1.0 + normed * (1.0 - sig))
        mean = jnp.sum(dn * normed, axis=1, keepdims=True) / c1
        return inv * (dn - normed * mean)

    low_ok = l > 0
    high_ok = l < n - 1
    for rr in range(3):
        seg[...] = jnp.dot(lx[...].reshape(rows, 1152), w1[:, rr * c1:(rr + 1) * c1], preferred_element_type=F32)
        normed, inv, hidden = norm(seg[...])
        if rr == 0:
            hidden = jnp.where(low_ok, hidden, 0.0)
        if rr == 2:
            hidden = jnp.where(high_ok, hidden, 0.0)
        spread(hidden, xc, rr, 2, False)
        if rr == 1:
            n1[...] = normed
            s1[...] = inv
            acc[...] = seg[...]

    copies[1].wait()

    def mid_tap(i, carry):
        a = i // 3
        b = i % 3
        left = xc[b, pl.ds(a, 4)].reshape(rows, 3 * c1)
        acc[...] += jnp.dot(left, wm[a, b].reshape(3 * c1, c1), preferred_element_type=F32)
        return carry

    lax.fori_loop(0, 9, mid_tap, 0)
    normed, inv, hidden = norm(acc[...])
    n2[...] = normed
    s2[...] = inv
    h2[1, pl.ds(2, 4)] = hidden.astype(BF).reshape(4, n, c1)
    mine = h2.at[1, pl.ds(2, 4)]
    h_copies = [
        remote(mine, h2.at[0, pl.ds(2, 4)], hs_s.at[0], hs_r.at[0], (s, nxt, c)),
        remote(mine, h2.at[2, pl.ds(2, 4)], hs_s.at[1], hs_r.at[1], (s, prv, c)),
    ]
    for copy in h_copies:
        copy.start()

    copies[2].wait()
    for copy in r_copies:
        copy.wait_recv()
    for i, edge in ((0, l == 0), (3, l == n - 1)):

        @pl.when(edge)
        def _():
            gb[:, i] = jnp.zeros_like(gb[:, i])

    for f in range(4):
        for b in range(3):
            first = lax.dot_general(bsel[...], gb[f, 2 - b].reshape(c2, 2 * n), NT, preferred_element_type=F32)
            second = lax.dot_general(bsel[...], gb[f, 3 - b].reshape(c2, 2 * n), NT, preferred_element_type=F32)
            pooled = (first + second).astype(BF)
            for e in range(3):
                sc[b, e, f] = pooled[e * n:(e + 1) * n]
    up[...] = jnp.zeros_like(up)

    def up_tap(i, carry):
        a = i // 3
        b = i % 3
        for e in range(3):
            left = sc[b, e, pl.ds(2 - a, 4)].reshape(rows, c2)
            up[...] += jnp.dot(left, wu[a, b, e], preferred_element_type=F32)
        return carry

    lax.fori_loop(0, 9, up_tap, 0)
    grad_two = norm_back(up[...], n2[...], s2[...])
    up[...] = grad_two
    g2[1] = grad_two.astype(BF).reshape(4, n, c1)
    g_copies = [
        remote(g2.at[1], g2.at[0], gs_s.at[0], gs_r.at[0], (s, nxt, c)),
        remote(g2.at[1], g2.at[2], gs_s.at[1], gs_r.at[1], (s, prv, c)),
    ]
    for copy in g_copies:
        copy.start()

    zero_pad = jnp.zeros((2, n, 3 * c1), BF)
    for rr in range(3):
        xc[rr, pl.ds(4, 2)] = zero_pad
    spread(grad_two.astype(BF).astype(F32), xc, 1, 0, True)
    acc[...] = jnp.zeros_like(acc)

    def back_tap(a, b):
        for e in range(3):
            left = xc[2 - b, pl.ds(2 - a, 4), :, pl.ds(e * c1, c1)].reshape(rows, c1)
            acc[...] += lax.dot_general(left, wm[a, b, e], NT, preferred_element_type=F32)

    def own_tap(a, carry):
        back_tap(a, 1)
        return carry

    lax.fori_loop(0, 3, own_tap, 0)
    for copy in g_copies:
        copy.wait_recv()
    for rr, ok in ((0, low_ok), (2, high_ok)):
        halo = g2[rr].reshape(rows, c1).astype(F32)
        spread(jnp.where(ok, halo, 0.0), xc, rr, 0, True)

    def halo_tap(i, carry):
        back_tap(i // 2, (i % 2) * 2)
        return carry

    lax.fori_loop(0, 6, halo_tap, 0)
    grad_one = up[...] + norm_back(acc[...], n1[...], s1[...])
    spread(grad_one.astype(BF).astype(F32), xc, 1, 0, True)
    total = jnp.zeros((n, 128), F32)
    for j in range(4):
        for e in range(3):
            left = xc[1, 2 * s + j, :, pl.ds(e * c1, c1)]
            total = total + lax.dot_general(left, wz[j, e], NT, preferred_element_type=F32)
    zs[...] = total.reshape(n, 1, 128)
    zr[l] = zs[l]

    def send_z(to):
        remote(zs.at[to], zr.at[l], zsem.at[0], zsem.at[1], (s, to, c)).start()

    each_partner(send_z)

    for copy in h_copies:
        copy.wait_recv()
    for rr, edge in ((0, l == 0), (2, l == n - 1)):

        @pl.when(edge)
        def _():
            h2[rr] = jnp.zeros_like(h2[rr])

    inter[...] = jnp.zeros_like(inter)
    col128 = lax.rem(lax.broadcasted_iota(jnp.int32, (2 * n, c2 // 2), 0), n)

    def dec_tap(a, carry):
        two = pl.ds(2 * s + a, 2)
        half = pl.ds(c * (c2 // 2), c2 // 2)
        for e in range(3):
            inter[e, pl.ds(0, rows)] += lax.dot_general(h2[0:2, two].reshape(rows, c1), wu[a, 0, e, half], NT, preferred_element_type=F32)
            inter[e, pl.ds(0, rows)] += lax.dot_general(h2[1:3, two].reshape(rows, c1), wu[a, 2, e, half], NT, preferred_element_type=F32)
            inter[e, pl.ds(rows, 2 * n)] += lax.dot_general(h2[1, two].reshape(2 * n, c1), wu[a, 1, e, half], NT, preferred_element_type=F32)
        return carry

    lax.fori_loop(0, 3, dec_tap, 0)
    for dy in range(2):
        by_tap = [inter[e, pl.ds(dy * 2 * n, 2 * n)] + inter[e, pl.ds(rows, 2 * n)] for e in range(3)]
        for dx in range(2):
            if dx == 0:
                full = shift_rows(by_tap[0], 1, col128, n) + by_tap[1] + by_tap[2]
            else:
                full = by_tap[0] + by_tap[1] + shift_rows(by_tap[2], -1, col128, n)
            for f in range(2):
                par[f, pl.ds(dx, n, stride=2), :] = full[f * n:(f + 1) * n]
        for f in range(2):
            dec_out[f, dy] = par[f].T.astype(BF)

    wait_bytes(zr.at[pl.ds(0, n - 1)], zsem.at[1])
    z = zr[...].reshape(n, 128)
    result = shift_rows(z, -1, row, n) + pltpu.roll(z, 128 - 32, axis=1) + pltpu.roll(shift_rows(z, 1, row, n), 128 - 64, axis=1)
    lg_out[...] = result.T[:32].reshape(2, 16, n)

    wait_bytes(view.at[:, pl.ds(0, n - 1)], la_s.at[0])
    wait_bytes(view, la_s.at[1])
    wait_bytes(zs.at[pl.ds(0, n - 1)], zsem.at[0])
    for copy in x_copies + r_copies + h_copies + g_copies:
        copy.wait_send()


def close_kernel(dec_in, lg_in, dec_out, lg_out):
    dec_out[...] = dec_in[...]
    lg_out[...] = lg_in[...]


def shards(n, latents, weight_in, weight_mid, weight_up, reward_grad):
    c1 = weight_mid.shape[4]
    c2 = weight_up.shape[4]
    rows = 4 * n
    vm = pltpu.VMEM
    dma = pltpu.SemaphoreType.DMA
    any_spec = pl.BlockSpec(memory_space=pl.ANY)
    vm_spec = pl.BlockSpec(memory_space=vm)
    decoded, grad = pl.pallas_call(
        functools.partial(kernel, n),
        out_shape=(
            jax.ShapeDtypeStruct((2, 2, c2 // 2, 2 * n), BF),
            jax.ShapeDtypeStruct((2, 16, n), F32),
        ),
        in_specs=[vm_spec, any_spec, any_spec, any_spec, any_spec],
        out_specs=(vm_spec, vm_spec),
        scratch_shapes=[
            vm((3, 3, 3, c1, c1), BF),
            vm((3, 3, 3, c2, c1), BF),
            vm((3, 3, 3, 16, c1), BF),
            vm((1152, 3 * c1), BF),
            vm((4, 3, 128, c1), BF),
            vm((3 * n, 2 * n), BF),
            vm((2, 2 * n, c2 // 2), F32),
            vm((4, 4, 2, c2 // 2, 2 * n), BF),
            vm((2, n, 1, 128), F32),
            vm((4, n, 1, 128), F32),
            vm((4, n, 1152), BF),
            vm((3, 6, n, 3 * c1), BF),
            vm((3, 6, n, c1), BF),
            vm((3, 4, n, c1), BF),
            vm((3, 3, 6, n, c2), BF),
            vm((rows, c1), F32),
            vm((rows, c1), F32),
            vm((rows, 1), F32),
            vm((rows, c1), F32),
            vm((rows, 1), F32),
            vm((rows, c1), F32),
            vm((n, 1, 128), F32),
            vm((n, 1, 128), F32),
            vm((rows, c1), F32),
            vm((3, 6 * n, c2 // 2), F32),
            dma((3,)), dma, dma((3,)), dma((3,)), dma((2,)), dma((2,)), dma((2,)), dma((2,)),
            dma((2,)), dma((2,)), dma((2,)), dma((2,)), dma((2,)),
        ],
        compiler_params=pltpu.CompilerParams(has_side_effects=True, collective_id=0, vmem_limit_bytes=60 * 1024 * 1024),
    )(latents.reshape(2, n, 16).transpose(0, 2, 1), reward_grad.transpose(0, 1, 3, 2), weight_in, weight_mid, weight_up.transpose(0, 1, 2, 4, 3))
    decoded, grad = pl.pallas_call(
        close_kernel,
        out_shape=(
            jax.ShapeDtypeStruct(decoded.shape, BF),
            jax.ShapeDtypeStruct(grad.shape, F32),
        ),
    )(decoded, grad)
    return decoded.transpose(0, 1, 3, 2), grad.transpose(0, 2, 1).reshape(2, n, 1, 16)


def solution(mesh):
    return jax.shard_map(
        functools.partial(shards, mesh.shape["slab"]),
        mesh=mesh,
        in_specs=(P("sec", None, "slab", None), P(), P(), P(), P("sec", "slab", None, "ch")),
        out_specs=(P("sec", "slab", None, "ch"), P("sec", None, "slab", None)),
        check_vma=False,
    )
```

```python
import functools

import jax
import jax.numpy as jnp
from jax import lax
from jax.experimental import pallas as pl
from jax.experimental.pallas import tpu as pltpu
from jax.sharding import PartitionSpec as P

EPSILON = 1e-06
MESH = pl.DeviceIdType.MESH
BF = jnp.bfloat16
F32 = jnp.float32
NT = (((1,), (1,)), ((), ()))


def shift_rows(x, step, col, width):
    rolled = pltpu.roll(x, step % x.shape[0], axis=0)
    if step > 0:
        return jnp.where(col < step, 0.0, rolled)
    return jnp.where(col >= width + step, 0.0, rolled)


def kernel(n, lat_in, rew_hbm, win_hbm, wm_hbm, wu_hbm, dec_out, lg_out,
           wm, wu, win, w1, wz, bsel, par, gb, view, lat, lx, xc, h2, g2, sc, seg, n1, s1, n2, s2, acc, zs, zr, up, inter,
           wsem, own_sem, xs_s, xs_r, rs_s, rs_r, la_s, la_r, hs_s, hs_r, gs_s, gs_r, zsem):
    s = lax.axis_index("sec")
    l = lax.axis_index("slab")
    c = lax.axis_index("ch")
    nxt = lax.rem(l + 1, n)
    prv = lax.rem(l + n - 1, n)
    rows = 4 * n
    c1 = wm.shape[3]
    c2 = wu.shape[3]

    copies = [
        pltpu.make_async_copy(win_hbm, win, wsem.at[0]),
        pltpu.make_async_copy(wm_hbm, wm, wsem.at[1]),
        pltpu.make_async_copy(wu_hbm, wu, wsem.at[2]),
    ]
    own = pltpu.make_async_copy(rew_hbm, gb.at[pl.ds(2 * s, 2), pl.ds(1, 2), c], own_sem)
    for copy in copies[:1] + [own] + copies[1:]:
        copy.start()

    barrier = pltpu.get_barrier_semaphore()

    def greet(ps, to, pc):
        pl.semaphore_signal(barrier, inc=1, device_id=(ps, to, pc), device_id_type=MESH)

    chunk = 9 if (n - 1) % 9 == 0 else n - 1

    def each_partner(act):
        def step(k, carry):
            for i in range(chunk):
                act(lax.rem(l + k * chunk + (1 + i), n))
            return carry

        lax.fori_loop(0, (n - 1) // chunk, step, 0)

    def greet_all(to):
        greet(s, to, c)
        greet(1 - s, to, c)

    peers = [(1 - s, c), (s, 1 - c), (1 - s, 1 - c)]
    for ps, pc in peers:
        greet(ps, l, pc)
    each_partner(greet_all)

    def remote(src, dst, ss, rs, dev):
        return pltpu.make_async_remote_copy(src_ref=src, dst_ref=dst, send_sem=ss, recv_sem=rs, device_id=dev, device_id_type=MESH)

    row = lax.broadcasted_iota(jnp.int32, (n, 128), 0)
    for f in range(2):
        x = jnp.concatenate([lat_in[f].astype(F32), jnp.zeros((16, 128 - n), F32)], axis=1)
        stack = [pltpu.roll(x, (2 - r) % 128, axis=1) if r != 2 else x for r in range(5)]
        both = jnp.concatenate(stack + [jnp.zeros((48, 128), F32)], axis=0)
        view[f] = both.T[:n].reshape(n, 1, 128)

    pick_row = lax.broadcasted_iota(jnp.int32, (n, 2 * n), 0)
    pick_col = lax.broadcasted_iota(jnp.int32, (n, 2 * n), 1)
    for e in range(3):
        delta = pick_col - 2 * pick_row - (1 - e)
        bsel[pl.ds(e * n, n)] = jnp.where((delta == 0) | (delta == 1), 1.0, 0.0).astype(BF)
    w1[...] = jnp.zeros_like(w1)
    wz[...] = jnp.zeros_like(wz)
    lx[...] = jnp.zeros_like(lx)
    h2[:, pl.ds(0, 2)] = jnp.zeros((3, 2, n, c1), BF)
    copies[0].wait()
    for a in range(3):
        for b in range(3):
            for e in range(3):
                piece = win[a, b, e]
                for rr in range(3):
                    w1[pl.ds((a * 3 + e) * 128 + 16 * (rr + b), 16), pl.ds(rr * c1, c1)] = piece
                for t in range(2):
                    j = t + 2 - a
                    wz[j, e, pl.ds(b * 32 + t * 16, 16), :] = piece
    for i in range(2):
        lat[2 * s + i, l] = view[i, l]

    pl.semaphore_wait(barrier, 2 * n + 1)

    def wait_bytes(ref, sem):
        pltpu.make_async_copy(ref, ref, sem).wait()

    x_copies = []
    for k, (ps, pc) in enumerate(peers):
        x_copies.append(remote(rew_hbm, gb.at[pl.ds(2 * s, 2), pl.ds(1, 2), c], xs_s.at[k], xs_r.at[k], (ps, l, pc)))
        x_copies[-1].start()

    def send_lat(to):
        remote(view.at[:, to], lat.at[pl.ds(2 * s, 2), l], la_s.at[0], la_r.at[0], (s, to, c)).start()
        remote(view.at[:, to], lat.at[pl.ds(2 * s, 2), l], la_s.at[1], la_r.at[1], (1 - s, to, c)).start()

    each_partner(send_lat)
    other = remote(view.at[:, l], lat.at[pl.ds(2 * s, 2), l], la_s.at[1], la_r.at[1], (1 - s, l, c))
    other.start()

    own.wait()
    for copy in x_copies:
        copy.wait_recv()
    r_copies = [
        remote(gb.at[:, 2], gb.at[:, 0], rs_s.at[0], rs_r.at[0], (s, nxt, c)),
        remote(gb.at[:, 1], gb.at[:, 3], rs_s.at[1], rs_r.at[1], (s, prv, c)),
    ]
    for copy in r_copies:
        copy.start()

    wait_bytes(lat.at[pl.ds(0, 2), pl.ds(0, n - 1)], la_r.at[0])
    wait_bytes(lat.at[pl.ds(0, 2)], la_r.at[1])

    for f in range(4):
        x = lat[f].reshape(n, 128)
        for e in range(3):
            moved = (shift_rows(x, 1 - e, row, n) if e != 1 else x).astype(BF)
            for a in range(3):
                t = f + 2 - a
                if t < 4:
                    lx[t, :, pl.ds((a * 3 + e) * 128, 128)] = moved
    big_col = lax.rem(lax.broadcasted_iota(jnp.int32, (rows, c1), 0), n)

    def spread(value, target, r, first, flip):
        for e in range(3):
            step = (e - 1) if flip else (1 - e)
            moved = shift_rows(value, step, big_col, n) if e != 1 else value
            target[r, pl.ds(first, 4), :, pl.ds(e * c1, c1)] = moved.astype(BF).reshape(4, n, c1)

    def norm(v):
        inv = lax.rsqrt(jnp.sum(v * v, axis=1, keepdims=True) / c1 + EPSILON)
        normed = v * inv
        return normed, inv, normed * jax.nn.sigmoid(normed)

    def norm_back(dh, normed, inv):
        sig = jax.nn.sigmoid(normed)
        dn = dh * sig * (1.0 + normed * (1.0 - sig))
        mean = jnp.sum(dn * normed, axis=1, keepdims=True) / c1
        return inv * (dn - normed * mean)

    low_ok = l > 0
    high_ok = l < n - 1
    for rr in range(3):
        seg[...] = jnp.dot(lx[...].reshape(rows, 1152), w1[:, rr * c1:(rr + 1) * c1], preferred_element_type=F32)
        normed, inv, hidden = norm(seg[...])
        if rr == 0:
            hidden = jnp.where(low_ok, hidden, 0.0)
        if rr == 2:
            hidden = jnp.where(high_ok, hidden, 0.0)
        spread(hidden, xc, rr, 2, False)
        if rr == 1:
            n1[...] = normed
            s1[...] = inv
            acc[...] = seg[...]

    copies[1].wait()

    def mid_taps(b, carry):
        for a in range(3):
            left = xc[b, pl.ds(2, 2 + a)].reshape((2 + a) * n, 3 * c1)
            part = pl.ds((2 - a) * n, (2 + a) * n)
            acc[part] += jnp.dot(left, wm[a, b].reshape(3 * c1, c1), preferred_element_type=F32)
        return carry

    lax.fori_loop(0, 3, mid_taps, 0)
    normed, inv, hidden = norm(acc[...])
    n2[...] = normed
    s2[...] = inv
    h2[1, pl.ds(2, 4)] = hidden.astype(BF).reshape(4, n, c1)
    mine = h2.at[1, pl.ds(2, 4)]
    h_copies = [
        remote(mine, h2.at[0, pl.ds(2, 4)], hs_s.at[0], hs_r.at[0], (s, nxt, c)),
        remote(mine, h2.at[2, pl.ds(2, 4)], hs_s.at[1], hs_r.at[1], (s, prv, c)),
    ]
    for copy in h_copies:
        copy.start()

    copies[2].wait()

    def pool(b):
        for f in range(4):
            first = lax.dot_general(bsel[...], gb[f, 2 - b].reshape(c2, 2 * n), NT, preferred_element_type=F32)
            second = lax.dot_general(bsel[...], gb[f, 3 - b].reshape(c2, 2 * n), NT, preferred_element_type=F32)
            pooled = (first + second).astype(BF)
            for e in range(3):
                sc[b, e, f] = pooled[e * n:(e + 1) * n]

    def up_taps(b):
        for a in range(3):
            for e in range(3):
                left = sc[b, e, pl.ds(2 - a, 2 + a)].reshape((2 + a) * n, c2)
                up[pl.ds(0, (2 + a) * n)] += jnp.dot(left, wu[a, b, e], preferred_element_type=F32)

    up[...] = jnp.zeros_like(up)
    pool(1)
    up_taps(1)
    for copy in r_copies:
        copy.wait_recv()
    for i, edge in ((0, l == 0), (3, l == n - 1)):

        @pl.when(edge)
        def _():
            gb[:, i] = jnp.zeros_like(gb[:, i])

    pool(0)
    pool(2)

    def edge_taps(i, carry):
        up_taps(2 * i)
        return carry

    lax.fori_loop(0, 2, edge_taps, 0)
    grad_two = norm_back(up[...], n2[...], s2[...])
    up[...] = grad_two
    g2[1] = grad_two.astype(BF).reshape(4, n, c1)
    g_copies = [
        remote(g2.at[1], g2.at[0], gs_s.at[0], gs_r.at[0], (s, nxt, c)),
        remote(g2.at[1], g2.at[2], gs_s.at[1], gs_r.at[1], (s, prv, c)),
    ]
    for copy in g_copies:
        copy.start()

    zero_pad = jnp.zeros((2, n, 3 * c1), BF)
    xc[1, pl.ds(4, 2)] = zero_pad
    spread(grad_two.astype(BF).astype(F32), xc, 1, 0, True)
    acc[...] = jnp.zeros_like(acc)

    def back_taps(b):
        for a in range(3):
            for e in range(3):
                left = xc[2 - b, pl.ds(2 - a, 2 + a), :, pl.ds(e * c1, c1)].reshape((2 + a) * n, c1)
                acc[pl.ds(0, (2 + a) * n)] += lax.dot_general(left, wm[a, b, e], NT, preferred_element_type=F32)

    back_taps(1)
    for copy in g_copies:
        copy.wait_recv()
    for rr, ok in ((0, low_ok), (2, high_ok)):
        halo = g2[rr].reshape(rows, c1).astype(F32)
        spread(jnp.where(ok, halo, 0.0), xc, rr, 0, True)

    def halo_taps(i, carry):
        back_taps(2 * i)
        return carry

    lax.fori_loop(0, 2, halo_taps, 0)
    grad_one = up[...] + norm_back(acc[...], n1[...], s1[...])
    spread(grad_one.astype(BF).astype(F32), xc, 1, 0, True)
    total = jnp.zeros((n, 128), F32)
    for j in range(4):
        for e in range(3):
            left = xc[1, 2 * s + j, :, pl.ds(e * c1, c1)]
            total = total + lax.dot_general(left, wz[j, e], NT, preferred_element_type=F32)
    zs[...] = total.reshape(n, 1, 128)
    zr[l] = zs[l]

    def send_z(to):
        remote(zs.at[to], zr.at[l], zsem.at[0], zsem.at[1], (s, to, c)).start()

    each_partner(send_z)

    for copy in h_copies:
        copy.wait_recv()
    for rr, edge in ((0, l == 0), (2, l == n - 1)):

        @pl.when(edge)
        def _():
            h2[rr] = jnp.zeros_like(h2[rr])

    inter[...] = jnp.zeros_like(inter)
    col128 = lax.rem(lax.broadcasted_iota(jnp.int32, (2 * n, c2 // 2), 0), n)

    def dec_tap(a, carry):
        two = pl.ds(2 * s + a, 2)
        half = pl.ds(c * (c2 // 2), c2 // 2)
        for e in range(3):
            inter[e, pl.ds(0, rows)] += lax.dot_general(h2[0:2, two].reshape(rows, c1), wu[a, 0, e, half], NT, preferred_element_type=F32)
            inter[e, pl.ds(0, rows)] += lax.dot_general(h2[1:3, two].reshape(rows, c1), wu[a, 2, e, half], NT, preferred_element_type=F32)
            inter[e, pl.ds(rows, 2 * n)] += lax.dot_general(h2[1, two].reshape(2 * n, c1), wu[a, 1, e, half], NT, preferred_element_type=F32)
        return carry

    lax.fori_loop(0, 3, dec_tap, 0)
    for dy in range(2):
        by_tap = [inter[e, pl.ds(dy * 2 * n, 2 * n)] + inter[e, pl.ds(rows, 2 * n)] for e in range(3)]
        for dx in range(2):
            if dx == 0:
                full = shift_rows(by_tap[0], 1, col128, n) + by_tap[1] + by_tap[2]
            else:
                full = by_tap[0] + by_tap[1] + shift_rows(by_tap[2], -1, col128, n)
            for f in range(2):
                par[f, pl.ds(dx, n, stride=2), :] = full[f * n:(f + 1) * n]
        for f in range(2):
            dec_out[f, dy] = par[f].T.astype(BF)

    wait_bytes(zr.at[pl.ds(0, n - 1)], zsem.at[1])
    z = zr[...].reshape(n, 128)
    result = shift_rows(z, -1, row, n) + pltpu.roll(z, 128 - 32, axis=1) + pltpu.roll(shift_rows(z, 1, row, n), 128 - 64, axis=1)
    lg_out[...] = result.T[:32].reshape(2, 16, n)

    wait_bytes(view.at[:, pl.ds(0, n - 1)], la_s.at[0])
    wait_bytes(view, la_s.at[1])
    wait_bytes(zs.at[pl.ds(0, n - 1)], zsem.at[0])
    for copy in x_copies + r_copies + h_copies + g_copies:
        copy.wait_send()


def close_kernel(dec_in, lg_in, dec_out, lg_out):
    dec_out[...] = dec_in[...]
    lg_out[...] = lg_in[...]


def shards(n, latents, weight_in, weight_mid, weight_up, reward_grad):
    c1 = weight_mid.shape[4]
    c2 = weight_up.shape[4]
    rows = 4 * n
    vm = pltpu.VMEM
    dma = pltpu.SemaphoreType.DMA
    any_spec = pl.BlockSpec(memory_space=pl.ANY)
    vm_spec = pl.BlockSpec(memory_space=vm)
    decoded, grad = pl.pallas_call(
        functools.partial(kernel, n),
        out_shape=(
            jax.ShapeDtypeStruct((2, 2, c2 // 2, 2 * n), BF),
            jax.ShapeDtypeStruct((2, 16, n), F32),
        ),
        in_specs=[vm_spec, any_spec, any_spec, any_spec, any_spec],
        out_specs=(vm_spec, vm_spec),
        scratch_shapes=[
            vm((3, 3, 3, c1, c1), BF),
            vm((3, 3, 3, c2, c1), BF),
            vm((3, 3, 3, 16, c1), BF),
            vm((1152, 3 * c1), BF),
            vm((4, 3, 128, c1), BF),
            vm((3 * n, 2 * n), BF),
            vm((2, 2 * n, c2 // 2), F32),
            vm((4, 4, 2, c2 // 2, 2 * n), BF),
            vm((2, n, 1, 128), F32),
            vm((4, n, 1, 128), F32),
            vm((4, n, 1152), BF),
            vm((3, 6, n, 3 * c1), BF),
            vm((3, 6, n, c1), BF),
            vm((3, 4, n, c1), BF),
            vm((3, 3, 6, n, c2), BF),
            vm((rows, c1), F32),
            vm((rows, c1), F32),
            vm((rows, 1), F32),
            vm((rows, c1), F32),
            vm((rows, 1), F32),
            vm((rows, c1), F32),
            vm((n, 1, 128), F32),
            vm((n, 1, 128), F32),
            vm((rows, c1), F32),
            vm((3, 6 * n, c2 // 2), F32),
            dma((3,)), dma, dma((3,)), dma((3,)), dma((2,)), dma((2,)), dma((2,)), dma((2,)),
            dma((2,)), dma((2,)), dma((2,)), dma((2,)), dma((2,)),
        ],
        compiler_params=pltpu.CompilerParams(has_side_effects=True, collective_id=0, vmem_limit_bytes=60 * 1024 * 1024),
    )(latents.reshape(2, n, 16).transpose(0, 2, 1), reward_grad.transpose(0, 1, 3, 2), weight_in, weight_mid, weight_up.transpose(0, 1, 2, 4, 3))
    decoded, grad = pl.pallas_call(
        close_kernel,
        out_shape=(
            jax.ShapeDtypeStruct(decoded.shape, BF),
            jax.ShapeDtypeStruct(grad.shape, F32),
        ),
    )(decoded, grad)
    return decoded.transpose(0, 1, 3, 2), grad.transpose(0, 2, 1).reshape(2, n, 1, 16)


def solution(mesh):
    return jax.shard_map(
        functools.partial(shards, mesh.shape["slab"]),
        mesh=mesh,
        in_specs=(P("sec", None, "slab", None), P(), P(), P(), P("sec", "slab", None, "ch")),
        out_specs=(P("sec", "slab", None, "ch"), P("sec", None, "slab", None)),
        check_vma=False,
    )
```

```python
import functools

import jax
import jax.numpy as jnp
from jax import lax
from jax.experimental import pallas as pl
from jax.experimental.pallas import tpu as pltpu
from jax.sharding import PartitionSpec as P

EPSILON = 1e-06
MESH = pl.DeviceIdType.MESH
BF = jnp.bfloat16
F32 = jnp.float32
NT = (((1,), (1,)), ((), ()))


def shift_rows(x, step, col, width):
    rolled = pltpu.roll(x, step % x.shape[0], axis=0)
    if step > 0:
        return jnp.where(col < step, 0.0, rolled)
    return jnp.where(col >= width + step, 0.0, rolled)


def kernel(n, lat_in, rew_hbm, win_hbm, wm_hbm, wu_hbm, dec_out, lg_out,
           wm, wu, win, w1, wz, bsel, par, gb, view, lat, lx, xc, h2, g2, sc, seg, n1, s1, n2, s2, acc, zs, zr, up, inter,
           wsem, own_sem, xs_s, xs_r, rs_s, rs_r, la_s, la_r, hs_s, hs_r, gs_s, gs_r, zsem):
    s = lax.axis_index("sec")
    l = lax.axis_index("slab")
    c = lax.axis_index("ch")
    nxt = lax.rem(l + 1, n)
    prv = lax.rem(l + n - 1, n)
    rows = 4 * n
    c1 = wm.shape[3]
    c2 = wu.shape[3]

    copies = [
        pltpu.make_async_copy(win_hbm, win, wsem.at[0]),
        pltpu.make_async_copy(wm_hbm, wm, wsem.at[1]),
        pltpu.make_async_copy(wu_hbm, wu, wsem.at[2]),
    ]
    own = pltpu.make_async_copy(rew_hbm, gb.at[pl.ds(2 * s, 2), pl.ds(1, 2), c], own_sem)
    for copy in copies[:1] + [own] + copies[1:]:
        copy.start()

    @pl.when(s == 1)
    def _():
        gb[pl.ds(0, 2), pl.ds(1, 2)] = jnp.zeros((2, 2, 2, c2 // 2, 2 * n), BF)

    barrier = pltpu.get_barrier_semaphore()

    def greet(ps, to, pc):
        pl.semaphore_signal(barrier, inc=1, device_id=(ps, to, pc), device_id_type=MESH)

    chunk = 9 if (n - 1) % 9 == 0 else n - 1

    def each_partner(act):
        def step(k, carry):
            for i in range(chunk):
                act(lax.rem(l + k * chunk + (1 + i), n))
            return carry

        lax.fori_loop(0, (n - 1) // chunk, step, 0)

    def greet_all(to):
        greet(s, to, c)
        greet(1 - s, to, c)

    peers = [(1 - s, c), (s, 1 - c), (1 - s, 1 - c)]
    for ps, pc in peers:
        greet(ps, l, pc)
    each_partner(greet_all)

    def remote(src, dst, ss, rs, dev):
        return pltpu.make_async_remote_copy(src_ref=src, dst_ref=dst, send_sem=ss, recv_sem=rs, device_id=dev, device_id_type=MESH)

    row = lax.broadcasted_iota(jnp.int32, (n, 128), 0)
    for f in range(2):
        x = jnp.concatenate([lat_in[f].astype(F32), jnp.zeros((16, 128 - n), F32)], axis=1)
        stack = [pltpu.roll(x, (2 - r) % 128, axis=1) if r != 2 else x for r in range(5)]
        both = jnp.concatenate(stack + [jnp.zeros((48, 128), F32)], axis=0)
        view[:, f] = both.T[:n].reshape(n, 1, 128)

    pick_row = lax.broadcasted_iota(jnp.int32, (n, 2 * n), 0)
    pick_col = lax.broadcasted_iota(jnp.int32, (n, 2 * n), 1)
    for e in range(3):
        delta = pick_col - 2 * pick_row - (1 - e)
        bsel[pl.ds(e * n, n)] = jnp.where((delta == 0) | (delta == 1), 1.0, 0.0).astype(BF)
    w1[...] = jnp.zeros_like(w1)
    wz[...] = jnp.zeros_like(wz)
    lx[...] = jnp.zeros_like(lx)
    h2[:, pl.ds(0, 2)] = jnp.zeros((3, 2, n, c1), BF)
    copies[0].wait()
    for a in range(3):
        for b in range(3):
            for e in range(3):
                piece = win[a, b, e]
                for rr in range(3):
                    w1[pl.ds((a * 3 + e) * 128 + 16 * (rr + b), 16), pl.ds(rr * c1, c1)] = piece
                for t in range(2):
                    j = t + 2 - a
                    wz[j, e, pl.ds(b * 32 + t * 16, 16), :] = piece
    lat[s, l] = view[l]

    pl.semaphore_wait(barrier, 2 * n + 1)

    def wait_bytes(ref, sem):
        pltpu.make_async_copy(ref, ref, sem).wait()

    x_copies = []
    for k, (ps, pc) in enumerate(peers):
        x_copies.append(remote(rew_hbm, gb.at[pl.ds(2 * s, 2), pl.ds(1, 2), c], xs_s.at[k], xs_r.at[k], (ps, l, pc)))

    @pl.when(s == 1)
    def _():
        x_copies[0].start()
        x_copies[2].start()

    x_copies[1].start()

    def send_lat(to):
        remote(view.at[to], lat.at[s, l], la_s.at[0], la_r.at[0], (s, to, c)).start()
        remote(view.at[to], lat.at[s, l], la_s.at[1], la_r.at[1], (1 - s, to, c)).start()

    each_partner(send_lat)
    other = remote(view.at[l], lat.at[s, l], la_s.at[1], la_r.at[1], (1 - s, l, c))
    other.start()

    own.wait()

    @pl.when(s == 0)
    def _():
        x_copies[0].wait_recv()
        x_copies[2].wait_recv()

    x_copies[1].wait_recv()
    r_copies = [
        remote(gb.at[:, 2], gb.at[:, 0], rs_s.at[0], rs_r.at[0], (s, nxt, c)),
        remote(gb.at[:, 1], gb.at[:, 3], rs_s.at[1], rs_r.at[1], (s, prv, c)),
    ]
    for copy in r_copies:
        copy.start()

    wait_bytes(lat.at[0, pl.ds(0, n - 1)], la_r.at[0])
    wait_bytes(lat.at[0], la_r.at[1])

    for f in range(4):
        x = lat[f // 2, :, f % 2].reshape(n, 128)
        for e in range(3):
            moved = (shift_rows(x, 1 - e, row, n) if e != 1 else x).astype(BF)
            for a in range(3):
                t = f + 2 - a
                if t < 4:
                    lx[t, :, pl.ds((a * 3 + e) * 128, 128)] = moved
    big_col = lax.rem(lax.broadcasted_iota(jnp.int32, (rows, c1), 0), n)

    def spread(value, target, r, first, flip):
        for e in range(3):
            step = (e - 1) if flip else (1 - e)
            moved = shift_rows(value, step, big_col, n) if e != 1 else value
            target[r, pl.ds(first, 4), :, pl.ds(e * c1, c1)] = moved.astype(BF).reshape(4, n, c1)

    def norm(v):
        inv = lax.rsqrt(jnp.sum(v * v, axis=1, keepdims=True) / c1 + EPSILON)
        normed = v * inv
        return normed, inv, normed * jax.nn.sigmoid(normed)

    def norm_back(dh, normed, inv):
        sig = jax.nn.sigmoid(normed)
        dn = dh * sig * (1.0 + normed * (1.0 - sig))
        mean = jnp.sum(dn * normed, axis=1, keepdims=True) / c1
        return inv * (dn - normed * mean)

    low_ok = l > 0
    high_ok = l < n - 1
    for rr in range(3):
        seg[...] = jnp.dot(lx[...].reshape(rows, 1152), w1[:, rr * c1:(rr + 1) * c1], preferred_element_type=F32)
        normed, inv, hidden = norm(seg[...])
        if rr == 0:
            hidden = jnp.where(low_ok, hidden, 0.0)
        if rr == 2:
            hidden = jnp.where(high_ok, hidden, 0.0)
        spread(hidden, xc, rr, 2, False)
        if rr == 1:
            n1[...] = normed
            s1[...] = inv
            acc[...] = seg[...]

    copies[1].wait()

    def mid_taps(b, carry):
        for a in range(3):
            left = xc[b, pl.ds(2, 2 + a)].reshape((2 + a) * n, 3 * c1)
            part = pl.ds((2 - a) * n, (2 + a) * n)
            acc[part] += jnp.dot(left, wm[a, b].reshape(3 * c1, c1), preferred_element_type=F32)
        return carry

    for i in range(3):
        mid_taps(i, 0)
    normed, inv, hidden = norm(acc[...])
    n2[...] = normed
    s2[...] = inv
    h2[1, pl.ds(2, 4)] = hidden.astype(BF).reshape(4, n, c1)
    mine = h2.at[1, pl.ds(2, 4)]
    h_copies = [
        remote(mine, h2.at[0, pl.ds(2, 4)], hs_s.at[0], hs_r.at[0], (s, nxt, c)),
        remote(mine, h2.at[2, pl.ds(2, 4)], hs_s.at[1], hs_r.at[1], (s, prv, c)),
    ]
    for copy in h_copies:
        copy.start()

    copies[2].wait()

    def pool(b):
        for f in range(4):
            first = lax.dot_general(bsel[...], gb[f, 2 - b].reshape(c2, 2 * n), NT, preferred_element_type=F32)
            second = lax.dot_general(bsel[...], gb[f, 3 - b].reshape(c2, 2 * n), NT, preferred_element_type=F32)
            pooled = (first + second).astype(BF)
            for e in range(3):
                sc[b, e, f] = pooled[e * n:(e + 1) * n]

    def up_taps(b):
        for a in range(3):
            for e in range(3):
                left = sc[b, e, pl.ds(2 - a, 2 + a)].reshape((2 + a) * n, c2)
                up[pl.ds(0, (2 + a) * n)] += jnp.dot(left, wu[a, b, e], preferred_element_type=F32)

    up[...] = jnp.zeros_like(up)
    pool(1)
    up_taps(1)
    for copy in r_copies:
        copy.wait_recv()
    for i, edge in ((0, l == 0), (3, l == n - 1)):

        @pl.when(edge)
        def _():
            gb[:, i] = jnp.zeros_like(gb[:, i])

    pool(0)
    pool(2)

    def edge_taps(i, carry):
        up_taps(2 * i)
        return carry

    for i in range(2):
        edge_taps(i, 0)
    grad_two = norm_back(up[...], n2[...], s2[...])
    up[...] = grad_two
    g2[1] = grad_two.astype(BF).reshape(4, n, c1)
    g_copies = [
        remote(g2.at[1], g2.at[0], gs_s.at[0], gs_r.at[0], (s, nxt, c)),
        remote(g2.at[1], g2.at[2], gs_s.at[1], gs_r.at[1], (s, prv, c)),
    ]
    for copy in g_copies:
        copy.start()

    zero_pad = jnp.zeros((2, n, 3 * c1), BF)
    xc[1, pl.ds(4, 2)] = zero_pad
    spread(grad_two.astype(BF).astype(F32), xc, 1, 0, True)
    acc[...] = jnp.zeros_like(acc)

    def back_taps(b):
        for a in range(3):
            for e in range(3):
                left = xc[2 - b, pl.ds(2 - a, 2 + a), :, pl.ds(e * c1, c1)].reshape((2 + a) * n, c1)
                acc[pl.ds(0, (2 + a) * n)] += lax.dot_general(left, wm[a, b, e], NT, preferred_element_type=F32)

    back_taps(1)
    for copy in g_copies:
        copy.wait_recv()
    for rr, ok in ((0, low_ok), (2, high_ok)):
        halo = g2[rr].reshape(rows, c1).astype(F32)
        spread(jnp.where(ok, halo, 0.0), xc, rr, 0, True)

    def halo_taps(i, carry):
        back_taps(2 * i)
        return carry

    for i in range(2):
        halo_taps(i, 0)
    grad_one = up[...] + norm_back(acc[...], n1[...], s1[...])
    spread(grad_one.astype(BF).astype(F32), xc, 1, 0, True)
    total = jnp.zeros((n, 128), F32)
    for j in range(4):
        for e in range(3):
            left = xc[1, 2 * s + j, :, pl.ds(e * c1, c1)]
            total = total + lax.dot_general(left, wz[j, e], NT, preferred_element_type=F32)
    zs[...] = total.reshape(n, 1, 128)
    zr[l] = zs[l]

    def send_z(to):
        remote(zs.at[to], zr.at[l], zsem.at[0], zsem.at[1], (s, to, c)).start()

    each_partner(send_z)

    for copy in h_copies:
        copy.wait_recv()
    for rr, edge in ((0, l == 0), (2, l == n - 1)):

        @pl.when(edge)
        def _():
            h2[rr] = jnp.zeros_like(h2[rr])

    inter[...] = jnp.zeros_like(inter)
    col128 = lax.rem(lax.broadcasted_iota(jnp.int32, (2 * n, c2 // 2), 0), n)

    def dec_tap(a, carry):
        two = pl.ds(2 * s + a, 2)
        half = pl.ds(c * (c2 // 2), c2 // 2)
        for e in range(3):
            inter[e, pl.ds(0, rows)] += lax.dot_general(h2[0:2, two].reshape(rows, c1), wu[a, 0, e, half], NT, preferred_element_type=F32)
            inter[e, pl.ds(0, rows)] += lax.dot_general(h2[1:3, two].reshape(rows, c1), wu[a, 2, e, half], NT, preferred_element_type=F32)
            inter[e, pl.ds(rows, 2 * n)] += lax.dot_general(h2[1, two].reshape(2 * n, c1), wu[a, 1, e, half], NT, preferred_element_type=F32)
        return carry

    lax.fori_loop(0, 3, dec_tap, 0)
    for dy in range(2):
        by_tap = [inter[e, pl.ds(dy * 2 * n, 2 * n)] + inter[e, pl.ds(rows, 2 * n)] for e in range(3)]
        for dx in range(2):
            if dx == 0:
                full = shift_rows(by_tap[0], 1, col128, n) + by_tap[1] + by_tap[2]
            else:
                full = by_tap[0] + by_tap[1] + shift_rows(by_tap[2], -1, col128, n)
            for f in range(2):
                par[f, pl.ds(dx, n, stride=2), :] = full[f * n:(f + 1) * n]
        for f in range(2):
            dec_out[f, dy] = par[f].T.astype(BF)

    wait_bytes(zr.at[pl.ds(0, n - 1)], zsem.at[1])
    z = zr[...].reshape(n, 128)
    result = shift_rows(z, -1, row, n) + pltpu.roll(z, 128 - 32, axis=1) + pltpu.roll(shift_rows(z, 1, row, n), 128 - 64, axis=1)
    lg_out[...] = result.T[:32].reshape(2, 16, n)

    wait_bytes(view.at[pl.ds(0, n - 1)], la_s.at[0])
    wait_bytes(view, la_s.at[1])
    wait_bytes(zs.at[pl.ds(0, n - 1)], zsem.at[0])
    @pl.when(s == 1)
    def _():
        x_copies[0].wait_send()
        x_copies[2].wait_send()

    for copy in x_copies[1:2] + r_copies + h_copies + g_copies:
        copy.wait_send()


def close_kernel(dec_in, lg_in, dec_out, lg_out):
    dec_out[...] = dec_in[...]
    lg_out[...] = lg_in[...]


def shards(n, latents, weight_in, weight_mid, weight_up, reward_grad):
    c1 = weight_mid.shape[4]
    c2 = weight_up.shape[4]
    rows = 4 * n
    vm = pltpu.VMEM
    dma = pltpu.SemaphoreType.DMA
    any_spec = pl.BlockSpec(memory_space=pl.ANY)
    vm_spec = pl.BlockSpec(memory_space=vm)
    decoded, grad = pl.pallas_call(
        functools.partial(kernel, n),
        out_shape=(
            jax.ShapeDtypeStruct((2, 2, c2 // 2, 2 * n), BF),
            jax.ShapeDtypeStruct((2, 16, n), F32),
        ),
        in_specs=[vm_spec, any_spec, any_spec, any_spec, any_spec],
        out_specs=(vm_spec, vm_spec),
        scratch_shapes=[
            vm((3, 3, 3, c1, c1), BF),
            vm((3, 3, 3, c2, c1), BF),
            vm((3, 3, 3, 16, c1), BF),
            vm((1152, 3 * c1), BF),
            vm((4, 3, 128, c1), BF),
            vm((3 * n, 2 * n), BF),
            vm((2, 2 * n, c2 // 2), F32),
            vm((4, 4, 2, c2 // 2, 2 * n), BF),
            vm((n, 2, 1, 128), F32),
            vm((2, n, 2, 1, 128), F32),
            vm((4, n, 1152), BF),
            vm((3, 6, n, 3 * c1), BF),
            vm((3, 6, n, c1), BF),
            vm((3, 4, n, c1), BF),
            vm((3, 3, 6, n, c2), BF),
            vm((rows, c1), F32),
            vm((rows, c1), F32),
            vm((rows, 1), F32),
            vm((rows, c1), F32),
            vm((rows, 1), F32),
            vm((rows, c1), F32),
            vm((n, 1, 128), F32),
            vm((n, 1, 128), F32),
            vm((rows, c1), F32),
            vm((3, 6 * n, c2 // 2), F32),
            dma((3,)), dma, dma((3,)), dma((3,)), dma((2,)), dma((2,)), dma((2,)), dma((2,)),
            dma((2,)), dma((2,)), dma((2,)), dma((2,)), dma((2,)),
        ],
        compiler_params=pltpu.CompilerParams(has_side_effects=True, collective_id=0, vmem_limit_bytes=60 * 1024 * 1024),
    )(latents.reshape(2, n, 16).transpose(0, 2, 1), reward_grad.transpose(0, 1, 3, 2), weight_in, weight_mid, weight_up.transpose(0, 1, 2, 4, 3))
    decoded, grad = pl.pallas_call(
        close_kernel,
        out_shape=(
            jax.ShapeDtypeStruct(decoded.shape, BF),
            jax.ShapeDtypeStruct(grad.shape, F32),
        ),
    )(decoded, grad)
    return decoded.transpose(0, 1, 3, 2), grad.transpose(0, 2, 1).reshape(2, n, 1, 16)


def solution(mesh):
    return jax.shard_map(
        functools.partial(shards, mesh.shape["slab"]),
        mesh=mesh,
        in_specs=(P("sec", None, "slab", None), P(), P(), P(), P("sec", "slab", None, "ch")),
        out_specs=(P("sec", "slab", None, "ch"), P("sec", None, "slab", None)),
        check_vma=False,
    )
```

```python
import functools

import jax
import jax.numpy as jnp
from jax import lax
from jax.experimental import pallas as pl
from jax.experimental.pallas import tpu as pltpu
from jax.sharding import PartitionSpec as P

EPSILON = 1e-06
MESH = pl.DeviceIdType.MESH
BF = jnp.bfloat16
F32 = jnp.float32
NT = (((1,), (1,)), ((), ()))


def shift_rows(x, step, col, width):
    rolled = pltpu.roll(x, step % x.shape[0], axis=0)
    if step > 0:
        return jnp.where(col < step, 0.0, rolled)
    return jnp.where(col >= width + step, 0.0, rolled)


def kernel(n, lat_in, rew_hbm, win_hbm, wm_hbm, wu_hbm, dec_out, lg_out,
           wm, wu, win, w1, wz, bsel, par, gb, view, lat, lx, xc, h2, g2, sc, seg, n1, s1, n2, s2, acc, zs, zr, up, inter,
           wsem, own_sem, xs_s, xs_r, rs_s, rs_r, la_s, la_r, hs_s, hs_r, gs_s, gs_r, zsem):
    s = lax.axis_index("sec")
    l = lax.axis_index("slab")
    c = lax.axis_index("ch")
    nxt = lax.rem(l + 1, n)
    prv = lax.rem(l + n - 1, n)
    rows = 4 * n
    c1 = wm.shape[3]
    c2 = wu.shape[3]

    copies = [
        pltpu.make_async_copy(win_hbm, win, wsem.at[0]),
        pltpu.make_async_copy(wm_hbm, wm, wsem.at[1]),
        pltpu.make_async_copy(wu_hbm, wu, wsem.at[2]),
    ]
    own = pltpu.make_async_copy(rew_hbm, gb.at[pl.ds(2 * s, 2), pl.ds(1, 2), c], own_sem)
    for copy in copies[:1] + [own] + copies[1:]:
        copy.start()

    @pl.when(s == 1)
    def _():
        gb[pl.ds(0, 2), pl.ds(1, 2)] = jnp.zeros((2, 2, 2, c2 // 2, 2 * n), BF)

    barrier = pltpu.get_barrier_semaphore()

    def greet(ps, to, pc):
        pl.semaphore_signal(barrier, inc=1, device_id=(ps, to, pc), device_id_type=MESH)

    def each_partner(act):
        act(lax.rem(l + n // 2, n))

        def step(d, carry):
            act(lax.rem(l + n // 2 - d, n))
            act(lax.rem(l + n // 2 + d, n))
            return carry

        lax.fori_loop(1, n // 2, step, 0)

    def greet_all(to):
        greet(s, to, c)
        greet(1 - s, to, c)

    peers = [(1 - s, c), (s, 1 - c), (1 - s, 1 - c)]
    each_partner(greet_all)
    for ps, pc in peers:
        greet(ps, l, pc)

    def remote(src, dst, ss, rs, dev):
        return pltpu.make_async_remote_copy(src_ref=src, dst_ref=dst, send_sem=ss, recv_sem=rs, device_id=dev, device_id_type=MESH)

    row = lax.broadcasted_iota(jnp.int32, (n, 128), 0)
    for f in range(2):
        x = jnp.concatenate([lat_in[f].astype(F32), jnp.zeros((16, 128 - n), F32)], axis=1)
        stack = [pltpu.roll(x, (2 - r) % 128, axis=1) if r != 2 else x for r in range(5)]
        both = jnp.concatenate(stack + [jnp.zeros((48, 128), F32)], axis=0)
        view[:, f] = both.T[:n].reshape(n, 1, 128)

    pick_row = lax.broadcasted_iota(jnp.int32, (n, 2 * n), 0)
    pick_col = lax.broadcasted_iota(jnp.int32, (n, 2 * n), 1)
    for e in range(3):
        delta = pick_col - 2 * pick_row - (1 - e)
        bsel[pl.ds(e * n, n)] = jnp.where((delta == 0) | (delta == 1), 1.0, 0.0).astype(BF)
    w1[...] = jnp.zeros_like(w1)
    wz[...] = jnp.zeros_like(wz)
    lx[...] = jnp.zeros_like(lx)
    h2[:, pl.ds(0, 2)] = jnp.zeros((3, 2, n, c1), BF)
    copies[0].wait()
    for a in range(3):
        for b in range(3):
            for e in range(3):
                piece = win[a, b, e]
                for rr in range(3):
                    w1[pl.ds((a * 3 + e) * 128 + 16 * (rr + b), 16), pl.ds(rr * c1, c1)] = piece
                for t in range(2):
                    j = t + 2 - a
                    wz[j, e, pl.ds(b * 32 + t * 16, 16), :] = piece
    lat[s, l] = view[l]

    pl.semaphore_wait(barrier, 2 * n + 1)

    def wait_bytes(ref, sem):
        pltpu.make_async_copy(ref, ref, sem).wait()

    x_copies = []
    for k, (ps, pc) in enumerate(peers):
        x_copies.append(remote(rew_hbm, gb.at[pl.ds(2 * s, 2), pl.ds(1, 2), c], xs_s.at[k], xs_r.at[k], (ps, l, pc)))

    @pl.when(s == 1)
    def _():
        x_copies[0].start()
        x_copies[2].start()

    x_copies[1].start()

    def send_lat(to):
        remote(view.at[to], lat.at[s, l], la_s.at[0], la_r.at[0], (s, to, c)).start()
        remote(view.at[to], lat.at[s, l], la_s.at[1], la_r.at[1], (1 - s, to, c)).start()

    each_partner(send_lat)
    other = remote(view.at[l], lat.at[s, l], la_s.at[1], la_r.at[1], (1 - s, l, c))
    other.start()

    own.wait()

    @pl.when(s == 0)
    def _():
        x_copies[0].wait_recv()
        x_copies[2].wait_recv()

    x_copies[1].wait_recv()
    r_copies = [
        remote(gb.at[:, 2], gb.at[:, 0], rs_s.at[0], rs_r.at[0], (s, nxt, c)),
        remote(gb.at[:, 1], gb.at[:, 3], rs_s.at[1], rs_r.at[1], (s, prv, c)),
    ]
    for copy in r_copies:
        copy.start()

    wait_bytes(lat.at[0, pl.ds(0, n - 1)], la_r.at[0])
    wait_bytes(lat.at[0], la_r.at[1])

    for f in range(4):
        x = lat[f // 2, :, f % 2].reshape(n, 128)
        for e in range(3):
            moved = (shift_rows(x, 1 - e, row, n) if e != 1 else x).astype(BF)
            for a in range(3):
                t = f + 2 - a
                if t < 4:
                    lx[t, :, pl.ds((a * 3 + e) * 128, 128)] = moved
    big_col = lax.rem(lax.broadcasted_iota(jnp.int32, (rows, c1), 0), n)

    def spread(value, target, r, first, flip):
        for e in range(3):
            step = (e - 1) if flip else (1 - e)
            moved = shift_rows(value, step, big_col, n) if e != 1 else value
            target[r, pl.ds(first, 4), :, pl.ds(e * c1, c1)] = moved.astype(BF).reshape(4, n, c1)

    def norm(v):
        inv = lax.rsqrt(jnp.sum(v * v, axis=1, keepdims=True) / c1 + EPSILON)
        normed = v * inv
        return normed, inv, normed * jax.nn.sigmoid(normed)

    def norm_back(dh, normed, inv):
        sig = jax.nn.sigmoid(normed)
        dn = dh * sig * (1.0 + normed * (1.0 - sig))
        mean = jnp.sum(dn * normed, axis=1, keepdims=True) / c1
        return inv * (dn - normed * mean)

    low_ok = l > 0
    high_ok = l < n - 1
    for rr in range(3):
        seg[...] = jnp.dot(lx[...].reshape(rows, 1152), w1[:, rr * c1:(rr + 1) * c1], preferred_element_type=F32)
        normed, inv, hidden = norm(seg[...])
        if rr == 0:
            hidden = jnp.where(low_ok, hidden, 0.0)
        if rr == 2:
            hidden = jnp.where(high_ok, hidden, 0.0)
        spread(hidden, xc, rr, 2, False)
        if rr == 1:
            n1[...] = normed
            s1[...] = inv
            acc[...] = seg[...]

    copies[1].wait()

    def mid_taps(b, carry):
        for a in range(3):
            left = xc[b, pl.ds(2, 2 + a)].reshape((2 + a) * n, 3 * c1)
            part = pl.ds((2 - a) * n, (2 + a) * n)
            acc[part] += jnp.dot(left, wm[a, b].reshape(3 * c1, c1), preferred_element_type=F32)
        return carry

    for i in range(3):
        mid_taps(i, 0)
    normed, inv, hidden = norm(acc[...])
    n2[...] = normed
    s2[...] = inv
    h2[1, pl.ds(2, 4)] = hidden.astype(BF).reshape(4, n, c1)
    mine = h2.at[1, pl.ds(2, 4)]
    h_copies = [
        remote(mine, h2.at[0, pl.ds(2, 4)], hs_s.at[0], hs_r.at[0], (s, nxt, c)),
        remote(mine, h2.at[2, pl.ds(2, 4)], hs_s.at[1], hs_r.at[1], (s, prv, c)),
    ]
    for copy in h_copies:
        copy.start()

    copies[2].wait()

    def pool(b):
        for f in range(4):
            first = lax.dot_general(bsel[...], gb[f, 2 - b].reshape(c2, 2 * n), NT, preferred_element_type=F32)
            second = lax.dot_general(bsel[...], gb[f, 3 - b].reshape(c2, 2 * n), NT, preferred_element_type=F32)
            pooled = (first + second).astype(BF)
            for e in range(3):
                sc[b, e, f] = pooled[e * n:(e + 1) * n]

    def up_taps(b):
        for a in range(3):
            for e in range(3):
                left = sc[b, e, pl.ds(2 - a, 2 + a)].reshape((2 + a) * n, c2)
                up[pl.ds(0, (2 + a) * n)] += jnp.dot(left, wu[a, b, e], preferred_element_type=F32)

    up[...] = jnp.zeros_like(up)
    pool(1)
    up_taps(1)
    for copy in r_copies:
        copy.wait_recv()
    for i, edge in ((0, l == 0), (3, l == n - 1)):

        @pl.when(edge)
        def _():
            gb[:, i] = jnp.zeros_like(gb[:, i])

    pool(0)
    pool(2)

    def edge_taps(i, carry):
        up_taps(2 * i)
        return carry

    for i in range(2):
        edge_taps(i, 0)
    grad_two = norm_back(up[...], n2[...], s2[...])
    up[...] = grad_two
    g2[1] = grad_two.astype(BF).reshape(4, n, c1)
    g_copies = [
        remote(g2.at[1], g2.at[0], gs_s.at[0], gs_r.at[0], (s, nxt, c)),
        remote(g2.at[1], g2.at[2], gs_s.at[1], gs_r.at[1], (s, prv, c)),
    ]
    for copy in g_copies:
        copy.start()

    zero_pad = jnp.zeros((2, n, 3 * c1), BF)
    xc[1, pl.ds(4, 2)] = zero_pad
    spread(grad_two.astype(BF).astype(F32), xc, 1, 0, True)
    acc[...] = jnp.zeros_like(acc)

    def back_taps(b):
        for a in range(3):
            for e in range(3):
                left = xc[2 - b, pl.ds(2 - a, 2 + a), :, pl.ds(e * c1, c1)].reshape((2 + a) * n, c1)
                acc[pl.ds(0, (2 + a) * n)] += lax.dot_general(left, wm[a, b, e], NT, preferred_element_type=F32)

    back_taps(1)
    for copy in g_copies:
        copy.wait_recv()
    for rr, ok in ((0, low_ok), (2, high_ok)):
        halo = g2[rr].reshape(rows, c1).astype(F32)
        spread(jnp.where(ok, halo, 0.0), xc, rr, 0, True)

    def halo_taps(i, carry):
        back_taps(2 * i)
        return carry

    for i in range(2):
        halo_taps(i, 0)
    grad_one = up[...] + norm_back(acc[...], n1[...], s1[...])
    spread(grad_one.astype(BF).astype(F32), xc, 1, 0, True)
    total = jnp.zeros((n, 128), F32)
    for j in range(4):
        for e in range(3):
            left = xc[1, 2 * s + j, :, pl.ds(e * c1, c1)]
            total = total + lax.dot_general(left, wz[j, e], NT, preferred_element_type=F32)
    zs[...] = total.reshape(n, 1, 128)
    zr[l] = zs[l]

    def send_z(to):
        remote(zs.at[to], zr.at[l], zsem.at[0], zsem.at[1], (s, to, c)).start()

    each_partner(send_z)

    for copy in h_copies:
        copy.wait_recv()
    for rr, edge in ((0, l == 0), (2, l == n - 1)):

        @pl.when(edge)
        def _():
            h2[rr] = jnp.zeros_like(h2[rr])

    inter[...] = jnp.zeros_like(inter)
    col128 = lax.rem(lax.broadcasted_iota(jnp.int32, (2 * n, c2 // 2), 0), n)

    def dec_tap(a, carry):
        two = pl.ds(2 * s + a, 2)
        half = pl.ds(c * (c2 // 2), c2 // 2)
        for e in range(3):
            inter[e, pl.ds(0, rows)] += lax.dot_general(h2[0:2, two].reshape(rows, c1), wu[a, 0, e, half], NT, preferred_element_type=F32)
            inter[e, pl.ds(0, rows)] += lax.dot_general(h2[1:3, two].reshape(rows, c1), wu[a, 2, e, half], NT, preferred_element_type=F32)
            inter[e, pl.ds(rows, 2 * n)] += lax.dot_general(h2[1, two].reshape(2 * n, c1), wu[a, 1, e, half], NT, preferred_element_type=F32)
        return carry

    lax.fori_loop(0, 3, dec_tap, 0)
    for dy in range(2):
        by_tap = [inter[e, pl.ds(dy * 2 * n, 2 * n)] + inter[e, pl.ds(rows, 2 * n)] for e in range(3)]
        for dx in range(2):
            if dx == 0:
                full = shift_rows(by_tap[0], 1, col128, n) + by_tap[1] + by_tap[2]
            else:
                full = by_tap[0] + by_tap[1] + shift_rows(by_tap[2], -1, col128, n)
            for f in range(2):
                par[f, pl.ds(dx, n, stride=2), :] = full[f * n:(f + 1) * n]
        for f in range(2):
            dec_out[f, dy] = par[f].T.astype(BF)

    wait_bytes(zr.at[pl.ds(0, n - 1)], zsem.at[1])
    z = zr[...].reshape(n, 128)
    result = shift_rows(z, -1, row, n) + pltpu.roll(z, 128 - 32, axis=1) + pltpu.roll(shift_rows(z, 1, row, n), 128 - 64, axis=1)
    lg_out[...] = result.T[:32].reshape(2, 16, n)

    wait_bytes(view.at[pl.ds(0, n - 1)], la_s.at[0])
    wait_bytes(view, la_s.at[1])
    wait_bytes(zs.at[pl.ds(0, n - 1)], zsem.at[0])
    @pl.when(s == 1)
    def _():
        x_copies[0].wait_send()
        x_copies[2].wait_send()

    for copy in x_copies[1:2] + r_copies + h_copies + g_copies:
        copy.wait_send()


def close_kernel(dec_in, lg_in, dec_out, lg_out):
    dec_out[...] = dec_in[...]
    lg_out[...] = lg_in[...]


def shards(n, latents, weight_in, weight_mid, weight_up, reward_grad):
    c1 = weight_mid.shape[4]
    c2 = weight_up.shape[4]
    rows = 4 * n
    vm = pltpu.VMEM
    dma = pltpu.SemaphoreType.DMA
    any_spec = pl.BlockSpec(memory_space=pl.ANY)
    vm_spec = pl.BlockSpec(memory_space=vm)
    decoded, grad = pl.pallas_call(
        functools.partial(kernel, n),
        out_shape=(
            jax.ShapeDtypeStruct((2, 2, c2 // 2, 2 * n), BF),
            jax.ShapeDtypeStruct((2, 16, n), F32),
        ),
        in_specs=[vm_spec, any_spec, any_spec, any_spec, any_spec],
        out_specs=(vm_spec, vm_spec),
        scratch_shapes=[
            vm((3, 3, 3, c1, c1), BF),
            vm((3, 3, 3, c2, c1), BF),
            vm((3, 3, 3, 16, c1), BF),
            vm((1152, 3 * c1), BF),
            vm((4, 3, 128, c1), BF),
            vm((3 * n, 2 * n), BF),
            vm((2, 2 * n, c2 // 2), F32),
            vm((4, 4, 2, c2 // 2, 2 * n), BF),
            vm((n, 2, 1, 128), F32),
            vm((2, n, 2, 1, 128), F32),
            vm((4, n, 1152), BF),
            vm((3, 6, n, 3 * c1), BF),
            vm((3, 6, n, c1), BF),
            vm((3, 4, n, c1), BF),
            vm((3, 3, 6, n, c2), BF),
            vm((rows, c1), F32),
            vm((rows, c1), F32),
            vm((rows, 1), F32),
            vm((rows, c1), F32),
            vm((rows, 1), F32),
            vm((rows, c1), F32),
            vm((n, 1, 128), F32),
            vm((n, 1, 128), F32),
            vm((rows, c1), F32),
            vm((3, 6 * n, c2 // 2), F32),
            dma((3,)), dma, dma((3,)), dma((3,)), dma((2,)), dma((2,)), dma((2,)), dma((2,)),
            dma((2,)), dma((2,)), dma((2,)), dma((2,)), dma((2,)),
        ],
        compiler_params=pltpu.CompilerParams(has_side_effects=True, collective_id=0, vmem_limit_bytes=60 * 1024 * 1024),
    )(latents.reshape(2, n, 16).transpose(0, 2, 1), reward_grad.transpose(0, 1, 3, 2), weight_in, weight_mid, weight_up.transpose(0, 1, 2, 4, 3))
    decoded, grad = pl.pallas_call(
        close_kernel,
        out_shape=(
            jax.ShapeDtypeStruct(decoded.shape, BF),
            jax.ShapeDtypeStruct(grad.shape, F32),
        ),
    )(decoded, grad)
    return decoded.transpose(0, 1, 3, 2), grad.transpose(0, 2, 1).reshape(2, n, 1, 16)


def solution(mesh):
    return jax.shard_map(
        functools.partial(shards, mesh.shape["slab"]),
        mesh=mesh,
        in_specs=(P("sec", None, "slab", None), P(), P(), P(), P("sec", "slab", None, "ch")),
        out_specs=(P("sec", "slab", None, "ch"), P("sec", None, "slab", None)),
        check_vma=False,
    )
```
